512 devices in a mesh: pair: 32 (over z, core), tau: 16 (over x, y).
Axes of the slice: x: 4, y: 4, z: 16, core: 2. Of those that a mesh axis runs over, the one named last changes fastest.
Arguments:
- coeff: bfloat16 [128, 128, 1024], P('pair'), may hold values from -6 to 6
- green_fwd: bfloat16 [1024, 16, 1024], P('pair', 'tau'), may hold values from -1 to 1
- green_bwd: bfloat16 [1024, 16, 1024], P('pair', 'tau'), may hold values from -1 to 1
- home_atom: int32 [1024], P('pair'), may hold values from 0 to 3, as said below
- send_atoms: int32 [1024], P('pair'), may hold values from 0 to 3, as said below
- partner: int32 [1024], P('pair'), may hold values from 0 to 31, as said below
- mirror: int32 [1024], P('pair'), may hold values from 0 to 1023, as said below
Outputs:
- response: float32 [1024, 16, 128, 128], P('pair', 'tau')
The draws below stay inside these ranges and needn't reach their ends.
Inputs may be any that keep to these rules, and one draw needn't show every extreme that they name: mirror[mirror[p]] = p for every pair; a pair's mirror has the same local number on its index of pair as the pair on its own; at most 1 pairs of one index of pair have their mirror on any one index of pair, and this is reached in every draw. partner[p] is the index of pair that holds mirror[p]. `home_atom`: the first atom of mirror[p] is the second atom of p, and the second atom of mirror[p] is the first atom of p. send_atoms[partner[p] * 32 + d] = home_atom[mirror[p]] for every pair p on index d of pair.
All inputs are finite; a program needn't handle non-finite values.
Results may differ from the reference program's by a relative error of at most 0.004.
Values may be sent and summed in bfloat16 or wider, within the bound.
No kernel may reach another device: no remote copies, remote signals or barrier semaphores. Data moves between devices by JAX's collectives and lax.ppermute only.
A program may use at most 64 MiB of HBM per device.

```python
import jax
import jax.numpy as jnp
from jax import lax

AUX = 128
AO = 32
ATOM_DEV = 4
PAIR_DEV = 32
ATOMS = 128
PAIRS = 1024
TAUS = 16
LINKS = 1024
N_PAIR = 32


def mirror_plan(key):
    masks = jax.random.permutation(jax.random.fold_in(key, 1), N_PAIR).astype(jnp.int32)
    table = jax.random.randint(jax.random.fold_in(key, 2), (N_PAIR, N_PAIR), 0, ATOM_DEV).astype(jnp.int32)
    return (masks, table)


def pair_layout():
    pair_index = jnp.arange(PAIRS, dtype=jnp.int32)
    device = pair_index // PAIR_DEV
    local_index = pair_index % PAIR_DEV
    return (device, local_index)


def draw_mirror(key, part):
    masks, table = mirror_plan(key)
    device, local_index = pair_layout()
    chosen = masks[local_index % N_PAIR]
    return (jnp.bitwise_xor(device, chosen) * PAIR_DEV + local_index).astype(jnp.int32)


def draw_partner(key, part):
    masks, table = mirror_plan(key)
    device, local_index = pair_layout()
    chosen = masks[local_index % N_PAIR]
    return jnp.bitwise_xor(device, chosen).astype(jnp.int32)


def draw_home_atom(key, part):
    masks, table = mirror_plan(key)
    device, local_index = pair_layout()
    return table[device, local_index % N_PAIR].astype(jnp.int32)


def draw_send_atoms(key, part):
    masks, table = mirror_plan(key)
    inverse = jnp.argsort(masks, stable=True).astype(jnp.int32)
    link_index = jnp.arange(LINKS, dtype=jnp.int32)
    owner = link_index // N_PAIR
    target = link_index % N_PAIR
    residue = inverse[jnp.bitwise_xor(owner, target)]
    return table[owner, residue].astype(jnp.int32)


def steps_of(rng, extent, cuts, low, high):
    factor_of, own = 1.0, jax.random.fold_in(rng, 6)
    for dim, parts in cuts:
        draws = jnp.exp(jax.random.uniform(jax.random.fold_in(own, dim), (parts,), jnp.float32, low / len(cuts), high / len(cuts)))
        factor_of = factor_of * jnp.repeat(draws, extent[dim] // parts).reshape([-1 if axis == dim else 1 for axis in range(len(extent))])
    return factor_of


def normal_values(rng, extent, spread, limit, cuts=(), kind=jnp.bfloat16):
    level = steps_of(rng, extent, cuts, -0.22, 0.18) if cuts else 1.0
    drawn = jax.random.normal(rng, extent, jnp.float32) * spread * level
    return jnp.minimum(jnp.maximum(drawn, -limit), limit).astype(kind)


def setup_inputs(seed: int = 0) -> dict:
    arg_keys = jax.random.split(jax.random.key(seed), 8)
    return {
        "coeff": normal_values(arg_keys[0], (ATOMS, AUX, AO * AO), 1.0, 6.0, ((0, 32),)),
        "green_fwd": normal_values(arg_keys[1], (PAIRS, TAUS, AO * AO), AO ** -0.5, 1.0, ((0, 32), (1, 16))),
        "green_bwd": normal_values(arg_keys[2], (PAIRS, TAUS, AO * AO), AO ** -0.5, 1.0, ((0, 32), (1, 16))),
        "home_atom": draw_home_atom(jax.random.fold_in(arg_keys[7], 71), 0),
        "send_atoms": draw_send_atoms(jax.random.fold_in(arg_keys[7], 71), 0),
        "partner": draw_partner(jax.random.fold_in(arg_keys[7], 71), 0),
        "mirror": draw_mirror(jax.random.fold_in(arg_keys[7], 71), 0),
    }


def pair_response(coeff_first, coeff_second, forward, backward):
    first_block = coeff_first.astype(jnp.float32).reshape(AUX, AO, AO)
    second_block = coeff_second.astype(jnp.float32).reshape(AUX, AO, AO)
    forward_tile = forward.astype(jnp.float32).reshape(-1, AO, AO)
    backward_tile = backward.astype(jnp.float32).reshape(-1, AO, AO)
    left_part = jnp.einsum('xac,tcb->txab', first_block, forward_tile).astype(jnp.bfloat16)
    right_part = jnp.einsum('tad,xdb->txab', backward_tile, second_block).astype(jnp.bfloat16)
    left_part = lax.optimization_barrier(left_part)
    right_part = lax.optimization_barrier(right_part)
    tau_count = forward_tile.shape[0]
    left_flat = left_part.astype(jnp.float32).reshape(tau_count, AUX, AO * AO)
    right_flat = right_part.astype(jnp.float32).reshape(tau_count, AUX, AO * AO)
    return jnp.einsum('txk,tyk->txy', left_flat, right_flat) * (1.0 / AO)


def reference(coeff, green_fwd, green_bwd, home_atom, send_atoms, partner, mirror):
    pair_index = jnp.arange(PAIRS, dtype=jnp.int32)
    device = pair_index // PAIR_DEV
    first_atom = (device * ATOM_DEV + home_atom).astype(jnp.int32)
    source = partner.astype(jnp.int32)
    second_atom = (source * ATOM_DEV + send_atoms[source * N_PAIR + device]).astype(jnp.int32)

    def one_pair(which):
        return pair_response(coeff[first_atom[which]], coeff[second_atom[which]], green_fwd[which], green_bwd[which])

    tiles = lax.map(one_pair, pair_index)
    return tiles + jnp.swapaxes(tiles[mirror], -1, -2)
```

```python
import jax
import jax.numpy as jnp
import numpy as np
from jax import lax
from jax.experimental import pallas as pl
from jax.experimental.pallas import tpu as pltpu
from jax.sharding import PartitionSpec as P

AUX = 128
AO = 32
F32 = jnp.float32
BF16 = jnp.bfloat16


def dot(a, b):
    return jnp.dot(a, b, preferred_element_type=F32)


def compute_kernel(home_ref, ci_ref, rb_ref, eg_ref, eh_ref, out_ref, st, cit, cjn, cjt, gw1, gw2, hm1, hm2):
    taus = 16
    ci = ci_ref[0]

    def swap_minor(src_rows):
        parts = [src_rows[pl.ds(w, AO, stride=AO), :] for w in range(AO)]
        return parts

    for c in range(8):
        st[pl.ds(c * 128, 128), :] = ci[:, c * 128:(c + 1) * 128].astype(F32).T
    for c in range(8):
        rows = jnp.concatenate([st[pl.ds(c * 4 + w, AO, stride=AO), :] for w in range(4)], axis=0)
        cit[:, c * 128:(c + 1) * 128] = rows.T.astype(BF16)
    cj = rb_ref[:, 0, :, :1024].astype(F32).reshape(AUX, 1024)
    for c in range(8):
        st[pl.ds(c * 128, 128), :] = cj[:, c * 128:(c + 1) * 128].T
    for c in range(4):
        cjn[:, c * 128:(c + 1) * 128] = st[pl.ds(c * 256, 256), :].astype(BF16)
    for w in range(AO):
        hi, lo = w // 8, w % 8
        cjt[lo * 32:(lo + 1) * 32, hi * 128:(hi + 1) * 128] = st[pl.ds(w, AO, stride=AO), :].astype(BF16)
    row32 = lax.broadcasted_iota(jnp.int32, (32, 128), 0) // 8
    lane32 = lax.broadcasted_iota(jnp.int32, (32, 128), 1) // 32
    keep = row32 == lane32
    eg = eg_ref[...]
    eh = eh_ref[...]

    def unpack(lo, e, dst):
        packed = rb_ref[:, 0, :, lo:lo + 128].astype(F32)
        rep = jnp.concatenate([packed] * 4, axis=1)
        rep = jnp.where(keep[None], rep, 0.0).reshape(taus * 32, 128).astype(BF16)
        dst[...] = dot(rep, e).reshape(taus, 32, 256)

    unpack(1024, eh, hm2)
    unpack(1152, eg, gw2)
    unpack(1280, eg, gw1)
    unpack(1408, eh, hm1)

    wrow = lax.broadcasted_iota(jnp.int32, (256, 256), 0)
    wlane = lax.broadcasted_iota(jnp.int32, (256, 256), 1)
    wmask = (wrow // 32) == (wlane % 8)
    mmask = ((wrow // 8) % 8) == (wlane // 32)

    def step(t, carry):
        g1 = gw1[t]
        g2 = gw2[t]
        h1 = hm1[t]
        h2 = hm2[t]

        def wide(g):
            return jnp.where(wmask, jnp.concatenate([g] * 8, axis=0), 0.0).astype(BF16)

        def tall(h):
            return jnp.where(
                mmask, jnp.concatenate([h[a * 8:(a + 1) * 8] for a in range(4) for _ in range(8)], axis=0), 0.0
            ).astype(BF16)

        w1, w2, m1, m2 = wide(g1), wide(g2), tall(h1), tall(h2)
        y1 = dot(m1, cjt[...]).astype(BF16)
        y2 = dot(m2, cjn[...]).astype(BF16)
        acc = jnp.zeros((AUX, AUX), F32)
        for c in range(4):
            cols = slice(c * 256, (c + 1) * 256)
            x1 = dot(ci_ref[0, :, cols], w1).astype(BF16)
            r1 = jnp.concatenate([y1[c * 64:(c + 1) * 64, h * 128:(h + 1) * 128] for h in range(4)], axis=0)
            acc = acc + dot(x1, r1)
            x2 = dot(cit[:, cols], w2).astype(BF16)
            r2 = jnp.concatenate([y2[c * 64:(c + 1) * 64, h * 128:(h + 1) * 128] for h in range(4)], axis=0)
            acc = acc + dot(x2, r2)
        out_ref[t, 0] = (acc * (1.0 / AO)).astype(BF16)
        return carry

    lax.fori_loop(0, taus, step, 0)


def expand_constants():
    i = np.arange(128)[:, None]
    j = np.arange(256)[None, :]
    eg = ((i % 32) == (j // 8)).astype(np.float32)
    eh = ((i % 32) == (j % 32)).astype(np.float32)
    return jnp.asarray(eg, BF16), jnp.asarray(eh, BF16)


def compute(home2, coeff, rb):
    eg, eh = expand_constants()
    taus = 16
    return pl.pallas_call(
        compute_kernel,
        grid_spec=pltpu.PrefetchScalarGridSpec(
            num_scalar_prefetch=1,
            grid=(2,),
            in_specs=[
                pl.BlockSpec((1, AUX, 1024), lambda m, home: (home[m], 0, 0)),
                pl.BlockSpec((taus, 1, 8, 1536), lambda m, home: (0, m, 0, 0)),
                pl.BlockSpec((128, 256), lambda m, home: (0, 0)),
                pl.BlockSpec((128, 256), lambda m, home: (0, 0)),
            ],
            out_specs=pl.BlockSpec((taus, 1, AUX, AUX), lambda m, home: (0, m, 0, 0)),
            scratch_shapes=[
                pltpu.VMEM((1024, 128), F32),
                pltpu.VMEM((128, 1024), BF16),
                pltpu.VMEM((256, 512), BF16),
                pltpu.VMEM((256, 512), BF16),
                pltpu.VMEM((taus, 32, 256), F32),
                pltpu.VMEM((taus, 32, 256), F32),
                pltpu.VMEM((taus, 32, 256), F32),
                pltpu.VMEM((taus, 32, 256), F32),
            ],
        ),
        out_shape=jax.ShapeDtypeStruct((taus, 2, AUX, AUX), BF16),
        cost_estimate=pl.CostEstimate(flops=26_000_000_000, bytes_accessed=3_000_000, transcendentals=0),
    )(home2, coeff, rb, eg, eh)


def body(coeff, green_fwd, green_bwd, home_atom, send_atoms, partner, mirror):
    taus = lax.axis_size("tau")
    k = lax.axis_index("tau")
    fwd = green_fwd[:, 0, :].reshape(32, 1, 1024)
    bwd = green_bwd[:, 0, :].reshape(32, 1, 1024)
    g = jnp.concatenate([fwd, bwd], axis=1)
    own = g.reshape(32, 2, 4, 8, 32).transpose(0, 3, 1, 2, 4).reshape(32, 8, 256)
    turned = g.reshape(32, 2, 32, 4, 8).transpose(0, 4, 1, 3, 2).reshape(32, 8, 256)
    index = jnp.arange(32, dtype=jnp.int32)
    inverse = jnp.sum(jnp.where(partner[None, :] == index[:, None], index[None, :], 0), axis=1)
    slices = lax.dynamic_slice(coeff, (0, k * 8, 0), (4, 8, 1024))
    send_a = jnp.concatenate(
        [jnp.take(slices, send_atoms, axis=0, mode="clip"), jnp.take(turned, inverse, axis=0, mode="clip")], axis=2
    )
    got_a = lax.all_to_all(send_a, "pair", split_axis=0, concat_axis=0, tiled=True)
    send_b = jnp.concatenate([jnp.take(got_a, partner, axis=0, mode="clip"), own], axis=2)
    got_b = lax.all_to_all(send_b, "tau", split_axis=0, concat_axis=0, tiled=True)
    home2 = lax.dynamic_slice(home_atom, (k * 2,), (2,))
    tiles = compute(home2, coeff, got_b.reshape(taus, 2, 8, 1536))
    back = lax.all_to_all(tiles.reshape(32, AUX, AUX), "tau", split_axis=0, concat_axis=0, tiled=True)
    return back.astype(F32).reshape(32, 1, AUX, AUX)


def solution(mesh):
    placed = (
        P("pair", None, None),
        P("pair", "tau", None),
        P("pair", "tau", None),
        P("pair"),
        P("pair"),
        P("pair"),
        P("pair"),
    )
    return jax.shard_map(
        body, mesh=mesh, in_specs=placed, out_specs=P("pair", "tau", None, None), check_vma=False
    )
```

```python
import jax
import jax.numpy as jnp
import numpy as np
from jax import lax
from jax.experimental import pallas as pl
from jax.experimental.pallas import tpu as pltpu
from jax.sharding import PartitionSpec as P

AUX = 128
AO = 32
CHIPS = 16
N_PAIR = 32
N_TAU = 16
F32 = jnp.float32
BF16 = jnp.bfloat16
BOTH = ("pair", "tau")


MATCH = (4, 15, 10, 5, 0, 3, 14, 9, 12, 7, 2, 13, 8, 11, 6, 1)


def routes():
    dst = np.zeros((N_PAIR, N_TAU, 2), np.int32)
    for z in range(CHIPS):
        for core in range(2):
            for k in range(N_TAU):
                dst[2 * z + core, k, 0] = 2 * ((5 * z + k) % CHIPS) + core
                dst[2 * z + core, k, 1] = 2 * ((5 * z + MATCH[k]) % CHIPS) + 1 - core
    src = np.zeros_like(dst)
    where = np.zeros((N_PAIR, N_PAIR), np.int32)
    for s in range(N_PAIR):
        for k in range(N_TAU):
            for j in range(2):
                d = dst[s, k, j]
                src[d, k, j] = s
                where[d, s] = 2 * k + j
    perms = [
        [(s * N_TAU + k, int(dst[s, k, j]) * N_TAU + k) for s in range(N_PAIR) for k in range(N_TAU)]
        for j in range(2)
    ]
    return dst, src, where, perms


DST, SRC, WHERE, PERMS = routes()


def dot(a, b):
    return jnp.dot(a, b, preferred_element_type=F32)


def z_kernel(home_ref, ci_ref, own_ref, far_ref, eg_ref, eh_ref, zt_ref, cin, f_own, f_far, b_own, b_far):
    for c in range(4):
        cin[:, c * 128:(c + 1) * 128] = ci_ref[0, :, c * 256:(c + 1) * 256].astype(F32).T.astype(BF16)
    keep = (lax.broadcasted_iota(jnp.int32, (64, 128), 0) // 16) == (lax.broadcasted_iota(jnp.int32, (64, 128), 1) // 32)

    def unpack(packed, e, dst):
        rep = jnp.concatenate([packed.astype(F32)] * 8, axis=1)
        rep = jnp.where(keep[None], rep, 0.0).reshape(N_TAU * 64, 128).astype(BF16)
        dst[...] = dot(rep, e).astype(BF16).reshape(N_TAU, 64, 256)

    unpack(own_ref[:, 0, :, 0:128], eh_ref[...], f_own)
    unpack(far_ref[:, :, 0:128], eh_ref[...], f_far)
    unpack(own_ref[:, 0, :, 128:256], eg_ref[...], b_own)
    unpack(far_ref[:, :, 128:256], eg_ref[...], b_far)
    row = lax.broadcasted_iota(jnp.int32, (64, 256), 0) // 8
    lane = lax.broadcasted_iota(jnp.int32, (64, 256), 1)
    mask_minor = jnp.where(row == lane // 32, 1.0, 0.0).astype(BF16)
    mask_major = jnp.where(row == lane % 8, 1.0, 0.0).astype(BF16)

    def spread(h, mask):
        return jnp.concatenate(
            [jnp.concatenate([h[a * 16:(a + 1) * 16]] * 4, axis=0) * mask for a in range(4)], axis=0
        )

    def half(f, b, t):
        s1 = dot(spread(f[t], mask_minor), cin[...]).astype(BF16)
        turned = jnp.concatenate(
            [
                jnp.concatenate([s1[h * 64:(h + 1) * 64, a * 128:(a + 1) * 128] for h in range(4)], axis=1)
                for a in range(4)
            ],
            axis=0,
        )
        return dot(spread(b[t], mask_major), turned)

    def step(t, carry):
        zt_ref[t] = (half(f_own, b_own, t) + half(f_far, b_far, t)).astype(BF16)
        return carry

    lax.fori_loop(0, N_TAU, step, 0)


def apply_z(slot, home, coeff, own, far, eg, eh):
    return pl.pallas_call(
        z_kernel,
        grid_spec=pltpu.PrefetchScalarGridSpec(
            num_scalar_prefetch=1,
            grid=(1,),
            in_specs=[
                pl.BlockSpec((1, AUX, 1024), lambda i, home: (home[0], 0, 0)),
                pl.BlockSpec((N_TAU, 1, 8, 256), lambda i, home: (0, slot, 0, 0)),
                pl.BlockSpec((N_TAU, 8, 256), lambda i, home: (0, 0, 0)),
                pl.BlockSpec((128, 256), lambda i, home: (0, 0)),
                pl.BlockSpec((128, 256), lambda i, home: (0, 0)),
            ],
            out_specs=pl.BlockSpec((N_TAU, 256, 512), lambda i, home: (0, 0, 0)),
            scratch_shapes=[pltpu.VMEM((256, 512), BF16)] + [pltpu.VMEM((N_TAU, 64, 256), BF16)] * 4,
        ),
        out_shape=jax.ShapeDtypeStruct((N_TAU, 256, 512), BF16),
        cost_estimate=pl.CostEstimate(flops=8_000_000_000, bytes_accessed=5_000_000, transcendentals=0),
    )(home, coeff, own, far, eg, eh)


def last_kernel(cj_ref, zt_ref, pm_ref, out_ref):
    turned = [dot(cj_ref[0, :, a * 256:(a + 1) * 256], pm_ref[...]) for a in range(4)]
    cjp = [
        jnp.concatenate([turned[a][:, h * 64:(h + 1) * 64] for a in range(4)], axis=1).astype(BF16) for h in range(4)
    ]
    for t in range(N_TAU):
        acc = dot(cjp[0], zt_ref[t, :, 0:128])
        for h in range(1, 4):
            acc = acc + dot(cjp[h], zt_ref[t, :, h * 128:(h + 1) * 128])
        out_ref[t] = (acc * (1.0 / AO)).astype(BF16)


def last_product(cj, zt, pm):
    return pl.pallas_call(
        last_kernel,
        out_shape=jax.ShapeDtypeStruct((N_TAU, AUX, AUX), BF16),
        cost_estimate=pl.CostEstimate(flops=600_000_000, bytes_accessed=5_000_000, transcendentals=0),
    )(cj, zt, pm)


def finish_kernel(place_ref, in_ref, out_ref):
    base = pl.program_id(0) * 8
    for i in range(8):
        out_ref[i] = in_ref[place_ref[base + i]].astype(F32).T


def finish(place, tiles):
    return pl.pallas_call(
        finish_kernel,
        grid_spec=pltpu.PrefetchScalarGridSpec(
            num_scalar_prefetch=1,
            grid=(4,),
            in_specs=[pl.BlockSpec((32, AUX, AUX), lambda i, place: (0, 0, 0))],
            out_specs=pl.BlockSpec((8, AUX, AUX), lambda i, place: (i, 0, 0)),
        ),
        out_shape=jax.ShapeDtypeStruct((32, AUX, AUX), F32),
        cost_estimate=pl.CostEstimate(flops=1_000_000, bytes_accessed=3_000_000, transcendentals=0),
    )(place, tiles)


def constants():
    i = np.arange(128)[:, None]
    j = np.arange(256)[None, :]
    eg = ((i % 32) == (j // 8)).astype(np.float32)
    eh = ((i % 32) == (j % 32)).astype(np.float32)
    r = np.arange(256)[:, None]
    lo, b = r // 32, r % 32
    pm = (j == (b // 8) * 64 + (b % 8) * 8 + lo).astype(np.float32)
    return jnp.asarray(eg, BF16), jnp.asarray(eh, BF16), jnp.asarray(pm, BF16)


def body(coeff, green_fwd, green_bwd, home_atom, send_atoms, partner, mirror):
    p = lax.axis_index("pair")
    k = lax.axis_index("tau")
    eg, eh, pm = constants()
    dst = jnp.asarray(DST)[p]
    src = jnp.asarray(SRC)[p]
    where = jnp.asarray(WHERE)[p]
    atoms = []
    for j in range(2):
        atom = lax.dynamic_index_in_dim(coeff, send_atoms[dst[k, j]], 0, keepdims=True)
        atoms.append(lax.ppermute(atom, BOTH, PERMS[j]))
    index = jnp.arange(N_PAIR, dtype=jnp.int32)
    inverse = jnp.sum(jnp.where(partner[None, :] == index[:, None], index[None, :], 0), axis=1)
    g = jnp.stack([green_fwd[:, 0, :], green_bwd[:, 0, :]], axis=1)
    plain = g.reshape(32, 2, 4, 8, 32).transpose(0, 3, 1, 2, 4).reshape(32, 8, 256)
    turned = g.reshape(32, 2, 32, 4, 8).transpose(0, 4, 1, 3, 2).reshape(32, 8, 256)
    own_rows = jnp.take(inverse, src.reshape(-1), mode="clip")
    far_rows = jnp.take(inverse, dst.reshape(-1), mode="clip")
    send = jnp.concatenate(
        [jnp.take(turned, own_rows, axis=0, mode="clip"), jnp.take(plain, far_rows, axis=0, mode="clip")], axis=2
    )
    greens = lax.all_to_all(send, "tau", split_axis=0, concat_axis=0, tiled=True).reshape(N_TAU, 2, 8, 512)
    far = [lax.ppermute(greens[:, j, :, 256:512], BOTH, PERMS[j]) for j in range(2)]
    home = [jnp.take(home_atom, own_rows, mode="clip").reshape(N_TAU, 2)[k, j].reshape(1) for j in range(2)]
    zts = [apply_z(j, home[j], coeff, greens, far[j], eg, eh) for j in range(2)]
    tiles = jnp.stack([last_product(atoms[j], zts[j], pm) for j in range(2)], axis=1)
    back = lax.all_to_all(tiles.reshape(32, AUX, AUX), "tau", split_axis=0, concat_axis=0, tiled=True)
    return finish(jnp.take(where, partner, mode="clip"), back).reshape(32, 1, AUX, AUX)


def solution(mesh):
    placed = (
        P("pair", None, None),
        P("pair", "tau", None),
        P("pair", "tau", None),
        P("pair"),
        P("pair"),
        P("pair"),
        P("pair"),
    )
    return jax.shard_map(
        body, mesh=mesh, in_specs=placed, out_specs=P("pair", "tau", None, None), check_vma=False
    )
```

```python
import functools

import jax
import jax.numpy as jnp
import numpy as np
from jax import lax
from jax.experimental import pallas as pl
from jax.experimental.pallas import tpu as pltpu
from jax.sharding import PartitionSpec as P


AUX = 128
AO = 32
CHIPS = 16
N_PAIR = 32
N_TAU = 16
F32 = jnp.float32
BF16 = jnp.bfloat16
BOTH = ("pair", "tau")


STEPS = (
    (1, 7, -7, -1), (7, -7, -1, 1), (-7, -1, 1, 7), (-1, 1, 7, -7),
    (2, -2, 6, -6), (-2, 2, -6, 6), (6, -6, 2, -2), (-6, 6, -2, 2),
    (3, -3, -5, 5), (-3, -5, 5, 3), (5, 3, -3, -5), (-5, 5, 3, -3),
    (0, 4, 8, -4), (4, 8, -4, 0), (8, -4, 0, 4), (-4, 0, 4, 8),
)


def routes():
    dst = np.zeros((CHIPS, N_TAU), np.int32)
    src = np.zeros((CHIPS, N_TAU), np.int32)
    column = np.zeros((CHIPS, CHIPS), np.int32)
    for z in range(CHIPS):
        for k in range(N_TAU):
            to = (z + STEPS[k][z % 4]) % CHIPS
            dst[z, k] = to
            src[to, k] = z
            column[to, z] = k
    along_z = [
        ((2 * z + core) * N_TAU + k, (2 * int(dst[z, k]) + core) * N_TAU + k)
        for z in range(CHIPS)
        for core in range(2)
        for k in range(N_TAU)
    ]
    return dst, src, column, along_z


DST, SRC, COLUMN, ALONG_Z = routes()
SWAP = [(i, i ^ 1) for i in range(N_PAIR)]


def dot(a, b):
    return jnp.dot(a, b, preferred_element_type=F32)


VM = pl.BlockSpec(memory_space=pltpu.VMEM)
SM = pl.BlockSpec(memory_space=pltpu.SMEM)


def prepare_kernel(
    spot_ref, partner_ref, asked_ref, homes_ref, dst_ref, src_ref, near_ref, away_ref, peers_ref, coeff_ref, gf_ref,
    gb_ref, send_ref, atom0_ref, atom1_ref, home_ref, wide
):
    p, k = spot_ref[0], spot_ref[1]
    z, core = p // 2, p % 2
    to = 2 * dst_ref[z * N_TAU + k]
    come = 2 * src_ref[z * N_TAU + k]
    for j, atom_ref in enumerate((atom0_ref, atom1_ref)):
        side = core if j == 0 else 1 - core
        atom_ref[0] = coeff_ref[asked_ref[to + side]]
        found = jnp.int32(0)
        for m in range(N_PAIR):
            found = jnp.where(partner_ref[m] == come + side, homes_ref[m], found)
        home_ref[j] = found
    eye = lax.broadcasted_iota(jnp.int32, (32, 32), 0) == lax.broadcasted_iota(jnp.int32, (32, 32), 1)
    peers = peers_ref[...]

    def pick(table_ref):
        row = table_ref[pl.ds(p, 1), :]
        column = jnp.sum(jnp.where(eye, jnp.broadcast_to(row, (32, 32)), 0.0), axis=1, keepdims=True)
        return jnp.where(column == peers, 1.0, 0.0).astype(BF16)

    near, away = pick(near_ref), pick(away_ref)
    mine = jnp.concatenate([dot(near, gf_ref[...]), dot(near, gb_ref[...])], axis=0).astype(BF16)
    theirs = [dot(away, gf_ref[...]), dot(away, gb_ref[...])]
    for c in range(4):
        r = lax.broadcasted_iota(jnp.int32, (1024, 256), 0)
        q = lax.broadcasted_iota(jnp.int32, (1, 256), 1) + 256 * c
        source = (q % 32) * 32 + ((q // 32) % 4) * 8 + q // 128
        turn = jnp.where(r == source, 1.0, 0.0).astype(BF16)
        flipped = dot(mine, turn)
        for i in range(2):
            for kind in range(2):
                wide[:, 2 * c + i, kind * 128:(kind + 1) * 128] = flipped[
                    kind * 32:(kind + 1) * 32, i * 128:(i + 1) * 128
                ]
    for kind in range(2):
        for lo in range(8):
            wide[:, lo, 256 + kind * 128:256 + (kind + 1) * 128] = jnp.concatenate(
                [theirs[kind][:, (hi * 8 + lo) * 32:(hi * 8 + lo + 1) * 32] for hi in range(4)], axis=1
            )
    send_ref[...] = wide[...].astype(BF16)


def prepare(spot, partner, send_atoms, home_atom, coeff, fwd, bwd):
    sides = np.arange(N_PAIR) % 2
    near = np.zeros((N_PAIR, N_PAIR), np.float32)
    away = np.zeros((N_PAIR, N_PAIR), np.float32)
    for p in range(N_PAIR):
        for j in range(2):
            near[p, j::2] = 2 * SRC[p // 2] + (sides[p] ^ j)
            away[p, j::2] = 2 * DST[p // 2] + (sides[p] ^ j)
    return pl.pallas_call(
        prepare_kernel,
        in_specs=[SM] * 6 + [VM] * 6,
        out_specs=[VM, VM, VM, SM],
        scratch_shapes=[pltpu.VMEM((32, 8, 512), F32)],
        out_shape=[
            jax.ShapeDtypeStruct((32, 8, 512), BF16),
            jax.ShapeDtypeStruct((1, AUX, 1024), BF16),
            jax.ShapeDtypeStruct((1, AUX, 1024), BF16),
            jax.ShapeDtypeStruct((2,), jnp.int32),
        ],
        cost_estimate=pl.CostEstimate(flops=200_000_000, bytes_accessed=3_000_000, transcendentals=0),
    )(
        spot,
        partner,
        send_atoms,
        home_atom,
        jnp.asarray(DST.reshape(-1)),
        jnp.asarray(SRC.reshape(-1)),
        jnp.asarray(near),
        jnp.asarray(away),
        partner.astype(F32).reshape(1, N_PAIR),
        coeff,
        fwd,
        bwd,
    )


UNROLL = 8


def z_kernel(slot, home_ref, ci_ref, own_ref, far_ref, eg_ref, eh_ref, z_ref, cin, fb, bb, s_a, s_b):
    for c in range(4):
        cin[:, c * 128:(c + 1) * 128] = ci_ref[home_ref[slot], :, c * 256:(c + 1) * 256].astype(F32).T.astype(BF16)
    keep = (lax.broadcasted_iota(jnp.int32, (64, 128), 0) // 16) == (lax.broadcasted_iota(jnp.int32, (64, 128), 1) // 32)

    def unpack(packed, e, dst, kind):
        rep = jnp.concatenate([packed.astype(F32)] * 8, axis=1)
        rep = jnp.where(keep[None], rep, 0.0).reshape(N_TAU * 64, 128).astype(BF16)
        dst[:, kind] = dot(rep, e).astype(BF16).reshape(N_TAU, 64, 256)

    unpack(own_ref[:, slot, :, 0:128], eh_ref[...], fb, 0)
    unpack(far_ref[0, :, :, 0:128], eh_ref[...], fb, 1)
    unpack(own_ref[:, slot, :, 128:256], eg_ref[...], bb, 0)
    unpack(far_ref[0, :, :, 128:256], eg_ref[...], bb, 1)
    row = lax.broadcasted_iota(jnp.int32, (64, 256), 0) // 8
    lane = lax.broadcasted_iota(jnp.int32, (64, 256), 1)
    mask_minor = jnp.where(row == lane // 32, 1.0, 0.0).astype(BF16)
    mask_major = jnp.where(row == lane % 8, 1.0, 0.0).astype(BF16)

    def spread(h, mask):
        return jnp.concatenate(
            [jnp.concatenate([h[a * 16:(a + 1) * 16]] * 4, axis=0) * mask for a in range(4)], axis=0
        )

    def first(t, buf):
        for kind in range(2):
            s1 = dot(spread(fb[t, kind], mask_minor), cin[...]).astype(BF16)
            for h in range(4):
                for a in range(4):
                    buf[kind * 256 + a * 64:kind * 256 + (a + 1) * 64, h * 128:(h + 1) * 128] = s1[
                        h * 64:(h + 1) * 64, a * 128:(a + 1) * 128
                    ]

    def second(t, buf):
        m2 = jnp.concatenate([spread(bb[t, 0], mask_major), spread(bb[t, 1], mask_major)], axis=1)
        for h in range(2):
            z = dot(m2, buf[:, h * 256:(h + 1) * 256])
            z_ref[t, :, h * 512:h * 512 + 256] = z[:, :128].T.astype(BF16)
            z_ref[t, :, h * 512 + 256:h * 512 + 512] = z[:, 128:].T.astype(BF16)

    first(0, s_a)

    def step(i, carry):
        for u in range(0, UNROLL, 2):
            t = UNROLL * i + u
            first(t + 1, s_b)
            second(t, s_a)
            first(jnp.minimum(t + 2, N_TAU - 1), s_a)
            second(t + 1, s_b)
        return carry

    lax.fori_loop(0, N_TAU // UNROLL, step, 0)


def apply_z(slot, home, coeff, own, far, eg, eh):
    return pl.pallas_call(
        functools.partial(z_kernel, slot),
        in_specs=[SM, VM, VM, VM, VM, VM],
        out_specs=VM,
        scratch_shapes=[pltpu.VMEM((256, 512), BF16)]
        + [pltpu.VMEM((N_TAU, 2, 64, 256), BF16)] * 2
        + [pltpu.VMEM((512, 512), BF16)] * 2,
        out_shape=jax.ShapeDtypeStruct((N_TAU, AUX, 1024), BF16),
        compiler_params=pltpu.CompilerParams(vmem_limit_bytes=16 * 2**20),
        cost_estimate=pl.CostEstimate(flops=8_000_000_000, bytes_accessed=5_000_000, transcendentals=0),
    )(home, coeff, own, far, eg, eh)


def last_kernel(c0_ref, c1_ref, z0_ref, z1_ref, pm_ref, out_ref, cp):
    for j, ref in enumerate((c0_ref, c1_ref)):
        turned = [dot(ref[0, :, a * 256:(a + 1) * 256], pm_ref[...]) for a in range(4)]
        for h in range(4):
            cp[j, :, h * 256:(h + 1) * 256] = jnp.concatenate(
                [turned[a][:, h * 64:(h + 1) * 64] for a in range(4)], axis=1
            ).astype(BF16)

    def step(i, carry):
        for j, ref in enumerate((z0_ref, z1_ref)):
            acc = lax.dot_general(
                ref[pl.ds(4 * i, 4)].reshape(4 * AUX, 1024),
                cp[j],
                (((1,), (1,)), ((), ())),
                preferred_element_type=F32,
            )
            out_ref[pl.ds(4 * i, 4), j] = (acc * (1.0 / AO)).astype(BF16).reshape(4, AUX, AUX)
        return carry

    lax.fori_loop(0, N_TAU // 4, step, 0)


def last_product(c0, c1, z0, z1, pm):
    return pl.pallas_call(
        last_kernel,
        in_specs=[VM] * 5,
        out_specs=VM,
        scratch_shapes=[pltpu.VMEM((2, AUX, 1024), BF16)],
        out_shape=jax.ShapeDtypeStruct((N_TAU, 2, AUX, AUX), BF16),
        compiler_params=pltpu.CompilerParams(vmem_limit_bytes=16 * 2**20),
        cost_estimate=pl.CostEstimate(flops=1_200_000_000, bytes_accessed=10_000_000, transcendentals=0),
    )(c0, c1, z0, z1, pm)


def finish_kernel(spot_ref, partner_ref, column_ref, in_ref, out_ref):
    base = pl.program_id(0) * 8
    p = spot_ref[0]
    for i in range(8):
        other = partner_ref[base + i]
        place = 2 * column_ref[(p // 2) * CHIPS + other // 2] + (p + other) % 2
        out_ref[i] = in_ref[place].astype(F32)


def finish(spot, partner, tiles):
    return pl.pallas_call(
        finish_kernel,
        grid=(4,),
        in_specs=[SM, SM, SM, VM],
        out_specs=pl.BlockSpec((8, AUX, AUX), lambda i: (i, 0, 0)),
        out_shape=jax.ShapeDtypeStruct((32, AUX, AUX), F32),
        compiler_params=pltpu.CompilerParams(vmem_limit_bytes=8 * 2**20),
        cost_estimate=pl.CostEstimate(flops=1_000_000, bytes_accessed=3_000_000, transcendentals=0),
    )(spot, partner, jnp.asarray(COLUMN.reshape(-1)), tiles)


def constants():
    i = np.arange(128)[:, None]
    j = np.arange(256)[None, :]
    eg = ((i % 32) == (j // 8)).astype(np.float32)
    eh = ((i % 32) == (j % 32)).astype(np.float32)
    r = np.arange(256)[:, None]
    lo, b = r // 32, r % 32
    pm = (j == (b // 8) * 64 + (b % 8) * 8 + lo).astype(np.float32)
    return jnp.asarray(eg, BF16), jnp.asarray(eh, BF16), jnp.asarray(pm, BF16)


def exchange(x):
    return lax.all_to_all(x, "tau", split_axis=0, concat_axis=0, tiled=True)


def body(coeff, green_fwd, green_bwd, home_atom, send_atoms, partner, mirror):
    spot = jnp.stack([lax.axis_index("pair"), lax.axis_index("tau")]).astype(jnp.int32)
    eg, eh, pm = constants()
    send, atom0, atom1, home = prepare(
        spot, partner, send_atoms, home_atom, coeff, green_fwd[:, 0, :], green_bwd[:, 0, :]
    )
    c0 = lax.ppermute(atom0, BOTH, ALONG_Z)
    greens = exchange(send).reshape(N_TAU, 2, 8, 512)
    outgoing, atom1 = lax.optimization_barrier((greens[:, :, :, 256:512].transpose(1, 0, 2, 3), atom1))
    far = lax.ppermute(outgoing, BOTH, ALONG_Z)
    other_far = lax.ppermute(far[1:2], "pair", SWAP)
    c1 = lax.ppermute(atom1, BOTH, ALONG_Z)
    c1 = lax.ppermute(c1, "pair", SWAP)
    z0 = apply_z(0, home, coeff, greens, far, eg, eh)
    z1 = apply_z(1, home, coeff, greens, other_far, eg, eh)
    tiles = last_product(c0, c1, z0, z1, pm)
    back = exchange(tiles.reshape(32, AUX, AUX))
    return finish(spot, partner, back).reshape(32, 1, AUX, AUX)


def solution(mesh):
    placed = (
        P("pair", None, None),
        P("pair", "tau", None),
        P("pair", "tau", None),
        P("pair"),
        P("pair"),
        P("pair"),
        P("pair"),
    )
    return jax.shard_map(
        body, mesh=mesh, in_specs=placed, out_specs=P("pair", "tau", None, None), check_vma=False
    )
```

```python
import functools

import jax
import jax.numpy as jnp
import numpy as np
from jax import lax
from jax.experimental import pallas as pl
from jax.experimental.pallas import tpu as pltpu
from jax.sharding import PartitionSpec as P


AUX = 128
AO = 32
CHIPS = 16
N_PAIR = 32
N_TAU = 16
F32 = jnp.float32
BF16 = jnp.bfloat16
BOTH = ("pair", "tau")


STEPS = (
    (1, 7, -7, -1), (7, -7, -1, 1), (-7, -1, 1, 7), (-1, 1, 7, -7),
    (2, -2, 6, -6), (-2, 2, -6, 6), (6, -6, 2, -2), (-6, 6, -2, 2),
    (3, -3, -5, 5), (-3, -5, 5, 3), (5, 3, -3, -5), (-5, 5, 3, -3),
    (0, 4, 8, -4), (4, 8, -4, 0), (8, -4, 0, 4), (-4, 0, 4, 8),
)


def routes():
    dst = np.zeros((CHIPS, N_TAU), np.int32)
    src = np.zeros((CHIPS, N_TAU), np.int32)
    column = np.zeros((CHIPS, CHIPS), np.int32)
    for z in range(CHIPS):
        for k in range(N_TAU):
            to = (z + STEPS[k][z % 4]) % CHIPS
            dst[z, k] = to
            src[to, k] = z
            column[to, z] = k
    along_z = [
        ((2 * z + core) * N_TAU + k, (2 * int(dst[z, k]) + core) * N_TAU + k)
        for z in range(CHIPS)
        for core in range(2)
        for k in range(N_TAU)
    ]
    return dst, src, column, along_z


DST, SRC, COLUMN, ALONG_Z = routes()
SWAP = [(i, i ^ 1) for i in range(N_PAIR)]


def dot(a, b):
    return jnp.dot(a, b, preferred_element_type=F32)


VM = pl.BlockSpec(memory_space=pltpu.VMEM)
SM = pl.BlockSpec(memory_space=pltpu.SMEM)


def prepare_kernel(
    asked_ref, dst_ref, near_ref, away_ref, peers_ref, coeff_ref, gf_ref, gb_ref, send_ref, atom0_ref, atom1a_ref,
    atom1b_ref, wide
):
    p, k = lax.axis_index("pair"), lax.axis_index("tau")
    z, core = p // 2, p % 2
    to = 2 * dst_ref[z * N_TAU + k]
    atom0_ref[0] = coeff_ref[asked_ref[to + core]]
    other = asked_ref[to + 1 - core]
    atom1a_ref[0] = coeff_ref[other, :64]
    atom1b_ref[0] = coeff_ref[other, 64:]
    eye = lax.broadcasted_iota(jnp.int32, (32, 32), 0) == lax.broadcasted_iota(jnp.int32, (32, 32), 1)
    peers = peers_ref[...].astype(F32)

    def pick(table_ref):
        row = table_ref[pl.ds(p, 1), :]
        column = jnp.sum(jnp.where(eye, jnp.broadcast_to(row, (32, 32)), 0.0), axis=1, keepdims=True)
        return jnp.where(column == peers, 1.0, 0.0).astype(BF16)

    near, away = pick(near_ref), pick(away_ref)
    mine = jnp.concatenate([dot(near, gf_ref[...]), dot(near, gb_ref[...])], axis=0).astype(BF16)
    theirs = [dot(away, gf_ref[...]), dot(away, gb_ref[...])]
    for c in range(4):
        r = lax.broadcasted_iota(jnp.int32, (1024, 256), 0)
        q = lax.broadcasted_iota(jnp.int32, (1, 256), 1) + 256 * c
        source = (q % 32) * 32 + ((q // 32) % 4) * 8 + q // 128
        turn = jnp.where(r == source, 1.0, 0.0).astype(BF16)
        flipped = dot(mine, turn)
        for i in range(2):
            for kind in range(2):
                wide[:, 2 * c + i, kind * 128:(kind + 1) * 128] = flipped[
                    kind * 32:(kind + 1) * 32, i * 128:(i + 1) * 128
                ]
    for kind in range(2):
        for lo in range(8):
            wide[:, lo, 256 + kind * 128:256 + (kind + 1) * 128] = jnp.concatenate(
                [theirs[kind][:, (hi * 8 + lo) * 32:(hi * 8 + lo + 1) * 32] for hi in range(4)], axis=1
            )
    send_ref[...] = wide[...].astype(BF16)


def prepare(partner, send_atoms, coeff, fwd, bwd):
    sides = np.arange(N_PAIR) % 2
    near = np.zeros((N_PAIR, N_PAIR), np.float32)
    away = np.zeros((N_PAIR, N_PAIR), np.float32)
    for p in range(N_PAIR):
        for j in range(2):
            near[p, j::2] = 2 * SRC[p // 2] + (sides[p] ^ j)
            away[p, j::2] = 2 * DST[p // 2] + (sides[p] ^ j)
    return pl.pallas_call(
        prepare_kernel,
        in_specs=[SM] * 2 + [VM] * 6,
        out_specs=[VM] * 4,
        scratch_shapes=[pltpu.VMEM((32, 8, 512), F32)],
        out_shape=[
            jax.ShapeDtypeStruct((32, 8, 512), BF16),
            jax.ShapeDtypeStruct((1, AUX, 1024), BF16),
            jax.ShapeDtypeStruct((1, 64, 1024), BF16),
            jax.ShapeDtypeStruct((1, 64, 1024), BF16),
        ],
        cost_estimate=pl.CostEstimate(flops=200_000_000, bytes_accessed=3_000_000, transcendentals=0),
    )(
        send_atoms,
        jnp.asarray(DST.reshape(-1)),
        jnp.asarray(near),
        jnp.asarray(away),
        partner.reshape(1, N_PAIR),
        coeff,
        fwd,
        bwd,
    )


def turn_kernel(partner_ref, homes_ref, src_ref, coeff_ref, cin_ref):
    p, k = lax.axis_index("pair"), lax.axis_index("tau")
    come = 2 * src_ref[(p // 2) * N_TAU + k]
    for j in range(2):
        side = (p + j) % 2
        home = jnp.int32(0)
        for m in range(N_PAIR):
            home = jnp.where(partner_ref[m] == come + side, homes_ref[m], home)
        for c in range(4):
            cin_ref[j, :, c * 128:(c + 1) * 128] = coeff_ref[home, :, c * 256:(c + 1) * 256].astype(F32).T.astype(BF16)


def turn_home(partner, home_atom, coeff):
    return pl.pallas_call(
        turn_kernel,
        in_specs=[SM] * 3 + [VM],
        out_specs=VM,
        out_shape=jax.ShapeDtypeStruct((2, 256, 512), BF16),
        cost_estimate=pl.CostEstimate(flops=100_000_000, bytes_accessed=2_000_000, transcendentals=0),
    )(partner, home_atom, jnp.asarray(SRC.reshape(-1)), coeff)


UNROLL = 8


def z_kernel(slot, cin_ref, own_ref, far_ref, z_ref, fb, bb, s_a, s_b):
    i = lax.broadcasted_iota(jnp.int32, (128, 256), 0) % 32
    j = lax.broadcasted_iota(jnp.int32, (128, 256), 1)
    eg = jnp.where(i == j // 8, 1.0, 0.0).astype(BF16)
    eh = jnp.where(i == j % 32, 1.0, 0.0).astype(BF16)
    keep = (lax.broadcasted_iota(jnp.int32, (64, 128), 0) // 16) == (lax.broadcasted_iota(jnp.int32, (64, 128), 1) // 32)

    def unpack(packed, e, dst, kind):
        rep = jnp.concatenate([packed.astype(F32)] * 8, axis=1)
        rep = jnp.where(keep[None], rep, 0.0).reshape(N_TAU * 64, 128).astype(BF16)
        dst[:, kind] = dot(rep, e).astype(BF16).reshape(N_TAU, 64, 256)

    unpack(own_ref[:, slot, :, 0:128], eh, fb, 0)
    unpack(far_ref[0, :, :, 0:128], eh, fb, 1)
    unpack(own_ref[:, slot, :, 128:256], eg, bb, 0)
    unpack(far_ref[0, :, :, 128:256], eg, bb, 1)
    row = lax.broadcasted_iota(jnp.int32, (64, 256), 0) // 8
    lane = lax.broadcasted_iota(jnp.int32, (64, 256), 1)
    mask_minor = jnp.where(row == lane // 32, 1.0, 0.0).astype(BF16)
    mask_major = jnp.where(row == lane % 8, 1.0, 0.0).astype(BF16)

    def spread(h, mask):
        return jnp.concatenate(
            [jnp.concatenate([h[a * 16:(a + 1) * 16]] * 4, axis=0) * mask for a in range(4)], axis=0
        )

    def first(t, buf):
        for kind in range(2):
            s1 = dot(spread(fb[t, kind], mask_minor), cin_ref[slot]).astype(BF16)
            for h in range(4):
                for a in range(4):
                    buf[kind * 256 + a * 64:kind * 256 + (a + 1) * 64, h * 128:(h + 1) * 128] = s1[
                        h * 64:(h + 1) * 64, a * 128:(a + 1) * 128
                    ]

    def second(t, buf):
        m2 = jnp.concatenate([spread(bb[t, 0], mask_major), spread(bb[t, 1], mask_major)], axis=1)
        for h in range(2):
            z = dot(m2, buf[:, h * 256:(h + 1) * 256])
            z_ref[t, :, h * 512:h * 512 + 256] = z[:, :128].T.astype(BF16)
            z_ref[t, :, h * 512 + 256:h * 512 + 512] = z[:, 128:].T.astype(BF16)

    first(0, s_a)

    def step(i, carry):
        for u in range(0, UNROLL, 2):
            t = UNROLL * i + u
            first(t + 1, s_b)
            second(t, s_a)
            first(jnp.minimum(t + 2, N_TAU - 1), s_a)
            second(t + 1, s_b)
        return carry

    lax.fori_loop(0, N_TAU // UNROLL, step, 0)


def apply_z(slot, cin, own, far):
    return pl.pallas_call(
        functools.partial(z_kernel, slot),
        in_specs=[VM] * 3,
        out_specs=VM,
        scratch_shapes=[pltpu.VMEM((N_TAU, 2, 64, 256), BF16)] * 2
        + [pltpu.VMEM((512, 512), BF16)] * 2,
        out_shape=jax.ShapeDtypeStruct((N_TAU, AUX, 1024), BF16),
        compiler_params=pltpu.CompilerParams(vmem_limit_bytes=16 * 2**20),
        cost_estimate=pl.CostEstimate(flops=8_000_000_000, bytes_accessed=5_000_000, transcendentals=0),
    )(cin, own, far)


def last_kernel(c0_ref, c1a_ref, c1b_ref, z0_ref, z1_ref, out_ref, cp):
    r = lax.broadcasted_iota(jnp.int32, (256, 256), 0)
    q = lax.broadcasted_iota(jnp.int32, (256, 256), 1)
    pm = jnp.where(q == (r % 32 // 8) * 64 + (r % 8) * 8 + r // 32, 1.0, 0.0).astype(BF16)
    for j in range(2):
        atom = c0_ref[0] if j == 0 else jnp.concatenate([c1a_ref[0], c1b_ref[0]], axis=0)
        turned = [dot(atom[:, a * 256:(a + 1) * 256], pm) for a in range(4)]
        for h in range(4):
            cp[j, :, h * 256:(h + 1) * 256] = jnp.concatenate(
                [turned[a][:, h * 64:(h + 1) * 64] for a in range(4)], axis=1
            ).astype(BF16)

    def step(i, carry):
        for j, ref in enumerate((z0_ref, z1_ref)):
            acc = lax.dot_general(
                ref[pl.ds(4 * i, 4)].reshape(4 * AUX, 1024),
                cp[j],
                (((1,), (1,)), ((), ())),
                preferred_element_type=F32,
            )
            out_ref[pl.ds(4 * i, 4), j] = (acc * (1.0 / AO)).astype(BF16).reshape(4, AUX, AUX)
        return carry

    lax.fori_loop(0, N_TAU // 4, step, 0)


def last_product(c0, c1a, c1b, z0, z1):
    return pl.pallas_call(
        last_kernel,
        in_specs=[VM] * 5,
        out_specs=VM,
        scratch_shapes=[pltpu.VMEM((2, AUX, 1024), BF16)],
        out_shape=jax.ShapeDtypeStruct((N_TAU, 2, AUX, AUX), BF16),
        compiler_params=pltpu.CompilerParams(vmem_limit_bytes=16 * 2**20),
        cost_estimate=pl.CostEstimate(flops=1_200_000_000, bytes_accessed=10_000_000, transcendentals=0),
    )(c0, c1a, c1b, z0, z1)


def finish_kernel(partner_ref, column_ref, in_ref, out_ref):
    base = pl.program_id(0) * 8
    p = lax.axis_index("pair")
    for i in range(8):
        other = partner_ref[base + i]
        place = 2 * column_ref[(p // 2) * CHIPS + other // 2] + (p + other) % 2
        out_ref[i] = in_ref[place].astype(F32)


def finish(partner, tiles):
    return pl.pallas_call(
        finish_kernel,
        grid=(4,),
        in_specs=[SM, SM, VM],
        out_specs=pl.BlockSpec((8, AUX, AUX), lambda i: (i, 0, 0)),
        out_shape=jax.ShapeDtypeStruct((32, AUX, AUX), F32),
        compiler_params=pltpu.CompilerParams(vmem_limit_bytes=8 * 2**20),
        cost_estimate=pl.CostEstimate(flops=1_000_000, bytes_accessed=3_000_000, transcendentals=0),
    )(partner, jnp.asarray(COLUMN.reshape(-1)), tiles)


def exchange(x):
    return lax.all_to_all(x, "tau", split_axis=0, concat_axis=0, tiled=True)


def send_z(x):
    return lax.ppermute(x, BOTH, ALONG_Z)


def swap(x):
    return lax.ppermute(x, "pair", SWAP)


def body(coeff, green_fwd, green_bwd, home_atom, send_atoms, partner, mirror):
    send, atom0, atom1a, atom1b = prepare(partner, send_atoms, coeff, green_fwd[:, 0, :], green_bwd[:, 0, :])
    greens = exchange(send).reshape(N_TAU, 2, 8, 512)
    c1a = send_z(atom1a)
    cin = turn_home(partner, home_atom, coeff)
    outgoing, atom0, atom1b = lax.optimization_barrier((greens[:, :, :, 256:512].transpose(1, 0, 2, 3), atom0, atom1b))
    far = send_z(outgoing)
    c1b = send_z(atom1b)
    c0 = send_z(atom0)
    z0 = apply_z(0, cin, greens, far)
    z1 = apply_z(1, cin, greens, swap(far[1:2]))
    tiles = last_product(c0, swap(c1a), swap(c1b), z0, z1)
    back = exchange(tiles.reshape(32, AUX, AUX))
    return finish(partner, back).reshape(32, 1, AUX, AUX)


def solution(mesh):
    placed = (
        P("pair", None, None),
        P("pair", "tau", None),
        P("pair", "tau", None),
        P("pair"),
        P("pair"),
        P("pair"),
        P("pair"),
    )
    return jax.shard_map(
        body, mesh=mesh, in_specs=placed, out_specs=P("pair", "tau", None, None), check_vma=False
    )
```

```python
import functools

import jax
import jax.numpy as jnp
import numpy as np
from jax import lax
from jax.experimental import pallas as pl
from jax.experimental.pallas import tpu as pltpu
from jax.sharding import PartitionSpec as P


AUX = 128
AO = 32
CHIPS = 16
N_PAIR = 32
N_TAU = 16
F32 = jnp.float32
BF16 = jnp.bfloat16
BOTH = ("pair", "tau")


STEPS = (
    (1, 7, -7, -1), (7, -7, -1, 1), (-7, -1, 1, 7), (-1, 1, 7, -7),
    (2, -2, 6, -6), (-2, 2, -6, 6), (6, -6, 2, -2), (-6, 6, -2, 2),
    (3, -3, -5, 5), (-3, -5, 5, 3), (5, 3, -3, -5), (-5, 5, 3, -3),
    (0, 4, 8, -4), (4, 8, -4, 0), (8, -4, 0, 4), (-4, 0, 4, 8),
)


def routes():
    dst = np.zeros((CHIPS, N_TAU), np.int32)
    src = np.zeros((CHIPS, N_TAU), np.int32)
    column = np.zeros((CHIPS, CHIPS), np.int32)
    for z in range(CHIPS):
        for k in range(N_TAU):
            to = (z + STEPS[k][z % 4]) % CHIPS
            dst[z, k] = to
            src[to, k] = z
            column[to, z] = k
    along_z = [
        ((2 * z + core) * N_TAU + k, (2 * int(dst[z, k]) + core) * N_TAU + k)
        for z in range(CHIPS)
        for core in range(2)
        for k in range(N_TAU)
    ]
    return dst, src, column, along_z


DST, SRC, COLUMN, ALONG_Z = routes()
SWAP = [(i, i ^ 1) for i in range(N_PAIR)]


def dot(a, b):
    return jnp.dot(a, b, preferred_element_type=F32)


VM = pl.BlockSpec(memory_space=pltpu.VMEM)
SM = pl.BlockSpec(memory_space=pltpu.SMEM)


def prepare_kernel(
    asked_ref, dst_ref, near_ref, away_ref, peers_ref, coeff_ref, gf_ref, gb_ref, send_ref, atoms_ref,
    wide
):
    p, k = lax.axis_index("pair"), lax.axis_index("tau")
    z, core = p // 2, p % 2
    to = 2 * dst_ref[z * N_TAU + k]
    atoms_ref[0] = coeff_ref[asked_ref[to + core]]
    atoms_ref[1] = coeff_ref[asked_ref[to + 1 - core]]
    eye = lax.broadcasted_iota(jnp.int32, (32, 32), 0) == lax.broadcasted_iota(jnp.int32, (32, 32), 1)
    peers = peers_ref[...].astype(F32)

    def pick(table_ref):
        row = table_ref[pl.ds(p, 1), :]
        column = jnp.sum(jnp.where(eye, jnp.broadcast_to(row, (32, 32)), 0.0), axis=1, keepdims=True)
        return jnp.where(column == peers, 1.0, 0.0).astype(BF16)

    near, away = pick(near_ref), pick(away_ref)
    mine = jnp.concatenate([dot(near, gf_ref[...]), dot(near, gb_ref[...])], axis=0).astype(BF16)
    theirs = [dot(away, gf_ref[...]), dot(away, gb_ref[...])]
    for c in range(4):
        r = lax.broadcasted_iota(jnp.int32, (1024, 256), 0)
        q = lax.broadcasted_iota(jnp.int32, (1, 256), 1) + 256 * c
        source = (q % 32) * 32 + ((q // 32) % 4) * 8 + q // 128
        turn = jnp.where(r == source, 1.0, 0.0).astype(BF16)
        flipped = dot(mine, turn)
        for i in range(2):
            for kind in range(2):
                wide[:, 2 * c + i, kind * 128:(kind + 1) * 128] = flipped[
                    kind * 32:(kind + 1) * 32, i * 128:(i + 1) * 128
                ]
    for kind in range(2):
        for lo in range(8):
            wide[:, lo, 256 + kind * 128:256 + (kind + 1) * 128] = jnp.concatenate(
                [theirs[kind][:, (hi * 8 + lo) * 32:(hi * 8 + lo + 1) * 32] for hi in range(4)], axis=1
            )
    send_ref[...] = wide[...].astype(BF16)


def prepare(partner, send_atoms, coeff, fwd, bwd):
    sides = np.arange(N_PAIR) % 2
    near = np.zeros((N_PAIR, N_PAIR), np.float32)
    away = np.zeros((N_PAIR, N_PAIR), np.float32)
    for p in range(N_PAIR):
        for j in range(2):
            near[p, j::2] = 2 * SRC[p // 2] + (sides[p] ^ j)
            away[p, j::2] = 2 * DST[p // 2] + (sides[p] ^ j)
    return pl.pallas_call(
        prepare_kernel,
        in_specs=[SM] * 2 + [VM] * 6,
        out_specs=[VM] * 2,
        scratch_shapes=[pltpu.VMEM((32, 8, 512), F32)],
        out_shape=[
            jax.ShapeDtypeStruct((32, 8, 512), BF16),
            jax.ShapeDtypeStruct((2, AUX, 1024), BF16),
        ],
        cost_estimate=pl.CostEstimate(flops=200_000_000, bytes_accessed=3_000_000, transcendentals=0),
    )(
        send_atoms,
        jnp.asarray(DST.reshape(-1)),
        jnp.asarray(near),
        jnp.asarray(away),
        partner.reshape(1, N_PAIR),
        coeff,
        fwd,
        bwd,
    )


def turn_kernel(partner_ref, homes_ref, src_ref, coeff_ref, cin_ref):
    p, k = lax.axis_index("pair"), lax.axis_index("tau")
    come = 2 * src_ref[(p // 2) * N_TAU + k]
    for j in range(2):
        side = (p + j) % 2
        home = jnp.int32(0)
        for m in range(N_PAIR):
            home = jnp.where(partner_ref[m] == come + side, homes_ref[m], home)
        for c in range(4):
            cin_ref[j, :, c * 128:(c + 1) * 128] = coeff_ref[home, :, c * 256:(c + 1) * 256].astype(F32).T.astype(BF16)


def turn_home(partner, home_atom, coeff):
    return pl.pallas_call(
        turn_kernel,
        in_specs=[SM] * 3 + [VM],
        out_specs=VM,
        out_shape=jax.ShapeDtypeStruct((2, 256, 512), BF16),
        cost_estimate=pl.CostEstimate(flops=100_000_000, bytes_accessed=2_000_000, transcendentals=0),
    )(partner, home_atom, jnp.asarray(SRC.reshape(-1)), coeff)


UNROLL = 8


def expand(packed, repeat, dst):
    rows = packed.shape[0]
    i = lax.broadcasted_iota(jnp.int32, (128, 256), 0) % 32
    j = lax.broadcasted_iota(jnp.int32, (128, 256), 1)
    e = jnp.where(i == (j // 8 if repeat else j % 32), 1.0, 0.0).astype(BF16)
    keep = (lax.broadcasted_iota(jnp.int32, (64, 128), 0) // 16) == (lax.broadcasted_iota(jnp.int32, (64, 128), 1) // 32)
    rep = jnp.concatenate([packed.astype(F32)] * 8, axis=1)
    rep = jnp.where(keep[None], rep, 0.0).reshape(rows * 64, 128).astype(BF16)
    dst[...] = dot(rep, e).astype(BF16).reshape(rows, 64, 256)


def pipelined(fb, bb, cin_of, emit, s_a, s_b):
    count = fb.shape[0]
    row = lax.broadcasted_iota(jnp.int32, (64, 256), 0) // 8
    lane = lax.broadcasted_iota(jnp.int32, (64, 256), 1)
    mask_minor = jnp.where(row == lane // 32, 1.0, 0.0).astype(BF16)
    mask_major = jnp.where(row == lane % 8, 1.0, 0.0).astype(BF16)

    def spread(h, mask):
        return jnp.concatenate(
            [jnp.concatenate([h[a * 16:(a + 1) * 16]] * 4, axis=0) * mask for a in range(4)], axis=0
        )

    def first(t, buf):
        s1 = dot(spread(fb[t], mask_minor), cin_of(t)).astype(BF16)
        for h in range(4):
            for a in range(4):
                buf[a * 64:(a + 1) * 64, h * 128:(h + 1) * 128] = s1[h * 64:(h + 1) * 64, a * 128:(a + 1) * 128]

    def second(t, buf):
        m2 = spread(bb[t], mask_major)
        for h in range(2):
            emit(t, h, dot(m2, buf[:, h * 256:(h + 1) * 256]))

    first(0, s_a)

    def step(i, carry):
        for u in range(0, UNROLL, 2):
            t = UNROLL * i + u
            first(t + 1, s_b)
            second(t, s_a)
            first(jnp.minimum(t + 2, count - 1), s_a)
            second(t + 1, s_b)
        return carry

    lax.fori_loop(0, count // UNROLL, step, 0)


def own_kernel(cin_ref, own_ref, zo_ref, fb, bb, s_a, s_b):
    for j in range(2):
        part = slice(j * N_TAU, (j + 1) * N_TAU)
        expand(own_ref[:, j, :, 0:128], False, fb.at[part])
        expand(own_ref[:, j, :, 128:256], True, bb.at[part])

    def emit(t, h, z):
        zo_ref[t, :, h * 256:(h + 1) * 256] = z

    pipelined(fb, bb, lambda t: cin_ref[t // N_TAU], emit, s_a, s_b)


def own_half(cin, greens):
    return pl.pallas_call(
        own_kernel,
        in_specs=[VM] * 2,
        out_specs=VM,
        scratch_shapes=[pltpu.VMEM((2 * N_TAU, 64, 256), BF16)] * 2 + [pltpu.VMEM((256, 512), BF16)] * 2,
        out_shape=jax.ShapeDtypeStruct((2 * N_TAU, 256, 512), F32),
        compiler_params=pltpu.CompilerParams(vmem_limit_bytes=24 * 2**20),
        cost_estimate=pl.CostEstimate(flops=8_000_000_000, bytes_accessed=5_000_000, transcendentals=0),
    )(cin, greens)


def far_kernel(slot, cin_ref, far_ref, zo_ref, z_ref, fb, bb, s_a, s_b):
    expand(far_ref[0, :, :, 0:128], False, fb)
    expand(far_ref[0, :, :, 128:256], True, bb)

    def emit(t, h, z):
        z = z + zo_ref[slot * N_TAU + t, :, h * 256:(h + 1) * 256]
        z_ref[t, :, h * 512:h * 512 + 256] = z[:, :128].T.astype(BF16)
        z_ref[t, :, h * 512 + 256:h * 512 + 512] = z[:, 128:].T.astype(BF16)

    pipelined(fb, bb, lambda t: cin_ref[slot], emit, s_a, s_b)


def far_half(slot, cin, far, zo):
    return pl.pallas_call(
        functools.partial(far_kernel, slot),
        in_specs=[VM] * 3,
        out_specs=VM,
        scratch_shapes=[pltpu.VMEM((N_TAU, 64, 256), BF16)] * 2 + [pltpu.VMEM((256, 512), BF16)] * 2,
        out_shape=jax.ShapeDtypeStruct((N_TAU, AUX, 1024), BF16),
        compiler_params=pltpu.CompilerParams(vmem_limit_bytes=24 * 2**20),
        cost_estimate=pl.CostEstimate(flops=4_000_000_000, bytes_accessed=5_000_000, transcendentals=0),
    )(cin, far, zo)


def last_kernel(c0_ref, c1_ref, z0_ref, z1_ref, out_ref, cp):
    r = lax.broadcasted_iota(jnp.int32, (256, 256), 0)
    q = lax.broadcasted_iota(jnp.int32, (256, 256), 1)
    pm = jnp.where(q == (r % 32 // 8) * 64 + (r % 8) * 8 + r // 32, 1.0, 0.0).astype(BF16)
    for j, ref in enumerate((c0_ref, c1_ref)):
        turned = [dot(ref[0, :, a * 256:(a + 1) * 256], pm) for a in range(4)]
        for h in range(4):
            cp[j, :, h * 256:(h + 1) * 256] = jnp.concatenate(
                [turned[a][:, h * 64:(h + 1) * 64] for a in range(4)], axis=1
            ).astype(BF16)

    def step(i, carry):
        for j, ref in enumerate((z0_ref, z1_ref)):
            acc = lax.dot_general(
                ref[pl.ds(4 * i, 4)].reshape(4 * AUX, 1024),
                cp[j],
                (((1,), (1,)), ((), ())),
                preferred_element_type=F32,
            )
            out_ref[pl.ds(4 * i, 4), j] = (acc * (1.0 / AO)).astype(BF16).reshape(4, AUX, AUX)
        return carry

    lax.fori_loop(0, N_TAU // 4, step, 0)


def last_product(c0, c1, z0, z1):
    return pl.pallas_call(
        last_kernel,
        in_specs=[VM] * 4,
        out_specs=VM,
        scratch_shapes=[pltpu.VMEM((2, AUX, 1024), BF16)],
        out_shape=jax.ShapeDtypeStruct((N_TAU, 2, AUX, AUX), BF16),
        compiler_params=pltpu.CompilerParams(vmem_limit_bytes=16 * 2**20),
        cost_estimate=pl.CostEstimate(flops=1_200_000_000, bytes_accessed=10_000_000, transcendentals=0),
    )(c0, c1, z0, z1)


def finish_kernel(partner_ref, column_ref, in_ref, out_ref):
    base = pl.program_id(0) * 8
    p = lax.axis_index("pair")
    for i in range(8):
        other = partner_ref[base + i]
        place = 2 * column_ref[(p // 2) * CHIPS + other // 2] + (p + other) % 2
        out_ref[i] = in_ref[place].astype(F32)


def finish(partner, tiles):
    return pl.pallas_call(
        finish_kernel,
        grid=(4,),
        in_specs=[SM, SM, VM],
        out_specs=pl.BlockSpec((8, AUX, AUX), lambda i: (i, 0, 0)),
        out_shape=jax.ShapeDtypeStruct((32, AUX, AUX), F32),
        compiler_params=pltpu.CompilerParams(vmem_limit_bytes=8 * 2**20),
        cost_estimate=pl.CostEstimate(flops=1_000_000, bytes_accessed=3_000_000, transcendentals=0),
    )(partner, jnp.asarray(COLUMN.reshape(-1)), tiles)


def exchange(x):
    return lax.all_to_all(x, "tau", split_axis=0, concat_axis=0, tiled=True)


def send_z(x):
    return lax.ppermute(x, BOTH, ALONG_Z)


def swap(x):
    return lax.ppermute(x, "pair", SWAP)


def body(coeff, green_fwd, green_bwd, home_atom, send_atoms, partner, mirror):
    send, atoms = prepare(partner, send_atoms, coeff, green_fwd[:, 0, :], green_bwd[:, 0, :])
    bulk = send_z(atoms)
    greens = exchange(send).reshape(N_TAU, 2, 8, 512)
    cin = turn_home(partner, home_atom, coeff)
    far = send_z(greens[:, :, :, 256:512].transpose(1, 0, 2, 3))
    zo = own_half(cin, greens)
    z0 = far_half(0, cin, far, zo)
    z1 = far_half(1, cin, swap(far[1:2]), zo)
    tiles = last_product(bulk, swap(bulk[1:2]), z0, z1)
    back = exchange(tiles.reshape(32, AUX, AUX))
    return finish(partner, back).reshape(32, 1, AUX, AUX)


def solution(mesh):
    placed = (
        P("pair", None, None),
        P("pair", "tau", None),
        P("pair", "tau", None),
        P("pair"),
        P("pair"),
        P("pair"),
        P("pair"),
    )
    return jax.shard_map(
        body, mesh=mesh, in_specs=placed, out_specs=P("pair", "tau", None, None), check_vma=False
    )
```

```python
import functools

import jax
import jax.numpy as jnp
import numpy as np
from jax import lax
from jax.experimental import pallas as pl
from jax.experimental.pallas import tpu as pltpu
from jax.sharding import PartitionSpec as P


AUX = 128
AO = 32
CHIPS = 16
N_PAIR = 32
N_TAU = 16
F32 = jnp.float32
BF16 = jnp.bfloat16
BOTH = ("pair", "tau")


STEPS = (
    (1, 7, -7, -1), (7, -7, -1, 1), (-7, -1, 1, 7), (-1, 1, 7, -7),
    (2, -2, 6, -6), (-2, 2, -6, 6), (6, -6, 2, -2), (-6, 6, -2, 2),
    (3, -3, -5, 5), (-3, -5, 5, 3), (5, 3, -3, -5), (-5, 5, 3, -3),
    (0, 4, 8, -4), (4, 8, -4, 0), (8, -4, 0, 4), (-4, 0, 4, 8),
)


def routes():
    dst = np.zeros((2, CHIPS, N_TAU), np.int32)
    src = np.zeros((2, CHIPS, N_TAU), np.int32)
    column = np.zeros((2, CHIPS, CHIPS), np.int32)
    perms = []
    for j in range(2):
        for z in range(CHIPS):
            for k in range(N_TAU):
                to = (z + STEPS[(k + 8 * j) % N_TAU][z % 4]) % CHIPS
                dst[j, z, k] = to
                src[j, to, k] = z
                column[j, to, z] = k
        perms.append(
            [
                ((2 * z + core) * N_TAU + k, (2 * int(dst[j, z, k]) + (core ^ j)) * N_TAU + k)
                for z in range(CHIPS)
                for core in range(2)
                for k in range(N_TAU)
            ]
        )
    return dst, src, column, perms


DST, SRC, COLUMN, PERMS = routes()


def dot(a, b):
    return jnp.dot(a, b, preferred_element_type=F32)


VM = pl.BlockSpec(memory_space=pltpu.VMEM)
SM = pl.BlockSpec(memory_space=pltpu.SMEM)


def prepare_kernel(
    asked_ref, dst_ref, near_ref, away_ref, peers_ref, coeff_ref, gf_ref, gb_ref, send_ref, atom0_ref,
    atom1_ref, wide
):
    p, k = lax.axis_index("pair"), lax.axis_index("tau")
    for j, atom_ref in enumerate((atom0_ref, atom1_ref)):
        to = 2 * dst_ref[(j * CHIPS + p // 2) * N_TAU + k] + (p + j) % 2
        atom_ref[0] = coeff_ref[asked_ref[to]]
    eye = lax.broadcasted_iota(jnp.int32, (32, 32), 0) == lax.broadcasted_iota(jnp.int32, (32, 32), 1)
    peers = peers_ref[...].astype(F32)

    def pick(table_ref):
        row = table_ref[pl.ds(p, 1), :]
        column = jnp.sum(jnp.where(eye, jnp.broadcast_to(row, (32, 32)), 0.0), axis=1, keepdims=True)
        return jnp.where(column == peers, 1.0, 0.0).astype(BF16)

    near, away = pick(near_ref), pick(away_ref)
    mine = jnp.concatenate([dot(near, gf_ref[...]), dot(near, gb_ref[...])], axis=0).astype(BF16)
    theirs = [dot(away, gf_ref[...]), dot(away, gb_ref[...])]
    for c in range(4):
        r = lax.broadcasted_iota(jnp.int32, (1024, 256), 0)
        q = lax.broadcasted_iota(jnp.int32, (1, 256), 1) + 256 * c
        source = (q % 32) * 32 + ((q // 32) % 4) * 8 + q // 128
        turn = jnp.where(r == source, 1.0, 0.0).astype(BF16)
        flipped = dot(mine, turn)
        for i in range(2):
            for kind in range(2):
                wide[:, 2 * c + i, kind * 128:(kind + 1) * 128] = flipped[
                    kind * 32:(kind + 1) * 32, i * 128:(i + 1) * 128
                ]
    for kind in range(2):
        for lo in range(8):
            wide[:, lo, 256 + kind * 128:256 + (kind + 1) * 128] = jnp.concatenate(
                [theirs[kind][:, (hi * 8 + lo) * 32:(hi * 8 + lo + 1) * 32] for hi in range(4)], axis=1
            )
    send_ref[...] = wide[...].astype(BF16)


def prepare(partner, send_atoms, coeff, fwd, bwd):
    sides = np.arange(N_PAIR) % 2
    near = np.zeros((N_PAIR, N_PAIR), np.float32)
    away = np.zeros((N_PAIR, N_PAIR), np.float32)
    for p in range(N_PAIR):
        for j in range(2):
            near[p, j::2] = 2 * SRC[j, p // 2] + (sides[p] ^ j)
            away[p, j::2] = 2 * DST[j, p // 2] + (sides[p] ^ j)
    return pl.pallas_call(
        prepare_kernel,
        in_specs=[SM] * 2 + [VM] * 6,
        out_specs=[VM] * 3,
        scratch_shapes=[pltpu.VMEM((32, 8, 512), F32)],
        out_shape=[
            jax.ShapeDtypeStruct((32, 8, 512), BF16),
            jax.ShapeDtypeStruct((1, AUX, 1024), BF16),
            jax.ShapeDtypeStruct((1, AUX, 1024), BF16),
        ],
        cost_estimate=pl.CostEstimate(flops=200_000_000, bytes_accessed=3_000_000, transcendentals=0),
    )(
        send_atoms,
        jnp.asarray(DST.reshape(-1)),
        jnp.asarray(near),
        jnp.asarray(away),
        partner.reshape(1, N_PAIR),
        coeff,
        fwd,
        bwd,
    )


def turn_kernel(partner_ref, homes_ref, src_ref, coeff_ref, cin_ref):
    p, k = lax.axis_index("pair"), lax.axis_index("tau")
    for j in range(2):
        come = 2 * src_ref[(j * CHIPS + p // 2) * N_TAU + k]
        side = (p + j) % 2
        home = jnp.int32(0)
        for m in range(N_PAIR):
            home = jnp.where(partner_ref[m] == come + side, homes_ref[m], home)
        for c in range(4):
            cin_ref[j, :, c * 128:(c + 1) * 128] = coeff_ref[home, :, c * 256:(c + 1) * 256].astype(F32).T.astype(BF16)


def turn_home(partner, home_atom, coeff):
    return pl.pallas_call(
        turn_kernel,
        in_specs=[SM] * 3 + [VM],
        out_specs=VM,
        out_shape=jax.ShapeDtypeStruct((2, 256, 512), BF16),
        cost_estimate=pl.CostEstimate(flops=100_000_000, bytes_accessed=2_000_000, transcendentals=0),
    )(partner, home_atom, jnp.asarray(SRC.reshape(-1)), coeff)


UNROLL = 8


def expand(packed, repeat, dst):
    rows = packed.shape[0]
    i = lax.broadcasted_iota(jnp.int32, (128, 256), 0) % 32
    j = lax.broadcasted_iota(jnp.int32, (128, 256), 1)
    e = jnp.where(i == (j // 8 if repeat else j % 32), 1.0, 0.0).astype(BF16)
    keep = (lax.broadcasted_iota(jnp.int32, (64, 128), 0) // 16) == (lax.broadcasted_iota(jnp.int32, (64, 128), 1) // 32)
    rep = jnp.concatenate([packed.astype(F32)] * 8, axis=1)
    rep = jnp.where(keep[None], rep, 0.0).reshape(rows * 64, 128).astype(BF16)
    dst[...] = dot(rep, e).astype(BF16).reshape(rows, 64, 256)


def pipelined(fb, bb, cin_of, emit, s_a, s_b):
    count = fb.shape[0]
    row = lax.broadcasted_iota(jnp.int32, (64, 256), 0) // 8
    lane = lax.broadcasted_iota(jnp.int32, (64, 256), 1)
    mask_minor = jnp.where(row == lane // 32, 1.0, 0.0).astype(BF16)
    mask_major = jnp.where(row == lane % 8, 1.0, 0.0).astype(BF16)

    def spread(h, mask):
        return jnp.concatenate(
            [jnp.concatenate([h[a * 16:(a + 1) * 16]] * 4, axis=0) * mask for a in range(4)], axis=0
        )

    def first(t, buf):
        s1 = dot(spread(fb[t], mask_minor), cin_of(t)).astype(BF16)
        for h in range(4):
            for a in range(4):
                buf[a * 64:(a + 1) * 64, h * 128:(h + 1) * 128] = s1[h * 64:(h + 1) * 64, a * 128:(a + 1) * 128]

    def second(t, buf):
        m2 = spread(bb[t], mask_major)
        for h in range(2):
            emit(t, h, dot(m2, buf[:, h * 256:(h + 1) * 256]))

    first(0, s_a)

    def step(i, carry):
        for u in range(0, UNROLL, 2):
            t = UNROLL * i + u
            first(t + 1, s_b)
            second(t, s_a)
            first(jnp.minimum(t + 2, count - 1), s_a)
            second(t + 1, s_b)
        return carry

    lax.fori_loop(0, count // UNROLL, step, 0)


def own_kernel(cin_ref, own_ref, zo_ref, fb, bb, s_a, s_b):
    for j in range(2):
        part = slice(j * N_TAU, (j + 1) * N_TAU)
        expand(own_ref[:, j, :, 0:128], False, fb.at[part])
        expand(own_ref[:, j, :, 128:256], True, bb.at[part])

    def emit(t, h, z):
        zo_ref[t, :, h * 256:(h + 1) * 256] = z

    pipelined(fb, bb, lambda t: cin_ref[t // N_TAU], emit, s_a, s_b)


def own_half(cin, greens):
    return pl.pallas_call(
        own_kernel,
        in_specs=[VM] * 2,
        out_specs=VM,
        scratch_shapes=[pltpu.VMEM((2 * N_TAU, 64, 256), BF16)] * 2 + [pltpu.VMEM((256, 512), BF16)] * 2,
        out_shape=jax.ShapeDtypeStruct((2 * N_TAU, 256, 512), F32),
        compiler_params=pltpu.CompilerParams(vmem_limit_bytes=24 * 2**20),
        cost_estimate=pl.CostEstimate(flops=8_000_000_000, bytes_accessed=5_000_000, transcendentals=0),
    )(cin, greens)


def far_kernel(slot, cin_ref, far_ref, zo_ref, z_ref, fb, bb, s_a, s_b):
    expand(far_ref[:, :, 0:128], False, fb)
    expand(far_ref[:, :, 128:256], True, bb)

    def emit(t, h, z):
        z = z + zo_ref[slot * N_TAU + t, :, h * 256:(h + 1) * 256]
        z_ref[t, :, h * 512:h * 512 + 256] = z[:, :128].T.astype(BF16)
        z_ref[t, :, h * 512 + 256:h * 512 + 512] = z[:, 128:].T.astype(BF16)

    pipelined(fb, bb, lambda t: cin_ref[slot], emit, s_a, s_b)


def far_half(slot, cin, far, zo):
    return pl.pallas_call(
        functools.partial(far_kernel, slot),
        in_specs=[VM] * 3,
        out_specs=VM,
        scratch_shapes=[pltpu.VMEM((N_TAU, 64, 256), BF16)] * 2 + [pltpu.VMEM((256, 512), BF16)] * 2,
        out_shape=jax.ShapeDtypeStruct((N_TAU, AUX, 1024), BF16),
        compiler_params=pltpu.CompilerParams(vmem_limit_bytes=24 * 2**20),
        cost_estimate=pl.CostEstimate(flops=4_000_000_000, bytes_accessed=5_000_000, transcendentals=0),
    )(cin, far, zo)


def last_kernel(c0_ref, c1_ref, z0_ref, z1_ref, out_ref, cp):
    r = lax.broadcasted_iota(jnp.int32, (256, 256), 0)
    q = lax.broadcasted_iota(jnp.int32, (256, 256), 1)
    pm = jnp.where(q == (r % 32 // 8) * 64 + (r % 8) * 8 + r // 32, 1.0, 0.0).astype(BF16)
    for j, ref in enumerate((c0_ref, c1_ref)):
        turned = [dot(ref[0, :, a * 256:(a + 1) * 256], pm) for a in range(4)]
        for h in range(4):
            cp[j, :, h * 256:(h + 1) * 256] = jnp.concatenate(
                [turned[a][:, h * 64:(h + 1) * 64] for a in range(4)], axis=1
            ).astype(BF16)

    def step(i, carry):
        for j, ref in enumerate((z0_ref, z1_ref)):
            acc = lax.dot_general(
                ref[pl.ds(4 * i, 4)].reshape(4 * AUX, 1024),
                cp[j],
                (((1,), (1,)), ((), ())),
                preferred_element_type=F32,
            )
            out_ref[pl.ds(4 * i, 4), j] = (acc * (1.0 / AO)).astype(BF16).reshape(4, AUX, AUX)
        return carry

    lax.fori_loop(0, N_TAU // 4, step, 0)


def last_product(c0, c1, z0, z1):
    return pl.pallas_call(
        last_kernel,
        in_specs=[VM] * 4,
        out_specs=VM,
        scratch_shapes=[pltpu.VMEM((2, AUX, 1024), BF16)],
        out_shape=jax.ShapeDtypeStruct((N_TAU, 2, AUX, AUX), BF16),
        compiler_params=pltpu.CompilerParams(vmem_limit_bytes=16 * 2**20),
        cost_estimate=pl.CostEstimate(flops=1_200_000_000, bytes_accessed=10_000_000, transcendentals=0),
    )(c0, c1, z0, z1)


def finish_kernel(partner_ref, column_ref, in_ref, out_ref):
    base = pl.program_id(0) * 8
    p = lax.axis_index("pair")
    for i in range(8):
        other = partner_ref[base + i]
        j = (p + other) % 2
        place = 2 * column_ref[(j * CHIPS + p // 2) * CHIPS + other // 2] + j
        out_ref[i] = in_ref[place].astype(F32)


def finish(partner, tiles):
    return pl.pallas_call(
        finish_kernel,
        grid=(4,),
        in_specs=[SM, SM, VM],
        out_specs=pl.BlockSpec((8, AUX, AUX), lambda i: (i, 0, 0)),
        out_shape=jax.ShapeDtypeStruct((32, AUX, AUX), F32),
        compiler_params=pltpu.CompilerParams(vmem_limit_bytes=8 * 2**20),
        cost_estimate=pl.CostEstimate(flops=1_000_000, bytes_accessed=3_000_000, transcendentals=0),
    )(partner, jnp.asarray(COLUMN.reshape(-1)), tiles)


def exchange(x):
    return lax.all_to_all(x, "tau", split_axis=0, concat_axis=0, tiled=True)


def send_z(x, j):
    return lax.ppermute(x, BOTH, PERMS[j])


def body(coeff, green_fwd, green_bwd, home_atom, send_atoms, partner, mirror):
    send, atom0, atom1 = prepare(partner, send_atoms, coeff, green_fwd[:, 0, :], green_bwd[:, 0, :])
    c0 = send_z(atom0, 0)
    c1 = send_z(atom1, 1)
    greens = exchange(send).reshape(N_TAU, 2, 8, 512)
    cin = turn_home(partner, home_atom, coeff)
    far0 = send_z(greens[:, 0, :, 256:512], 0)
    far1 = send_z(greens[:, 1, :, 256:512], 1)
    zo = own_half(cin, greens)
    z0 = far_half(0, cin, far0, zo)
    z1 = far_half(1, cin, far1, zo)
    tiles = last_product(c0, c1, z0, z1)
    back = exchange(tiles.reshape(32, AUX, AUX))
    return finish(partner, back).reshape(32, 1, AUX, AUX)


def solution(mesh):
    placed = (
        P("pair", None, None),
        P("pair", "tau", None),
        P("pair", "tau", None),
        P("pair"),
        P("pair"),
        P("pair"),
        P("pair"),
    )
    return jax.shard_map(
        body, mesh=mesh, in_specs=placed, out_specs=P("pair", "tau", None, None), check_vma=False
    )
```

```python
import functools

import jax
import jax.numpy as jnp
import numpy as np
from jax import lax
from jax.experimental import pallas as pl
from jax.experimental.pallas import tpu as pltpu
from jax.sharding import PartitionSpec as P


AUX = 128
AO = 32
CHIPS = 16
N_PAIR = 32
N_TAU = 16
F32 = jnp.float32
BF16 = jnp.bfloat16
BOTH = ("pair", "tau")


STEPS = (
    (1, 7, -7, -1), (7, -7, -1, 1), (-7, -1, 1, 7), (-1, 1, 7, -7),
    (2, -2, 6, -6), (-2, 2, -6, 6), (6, -6, 2, -2), (-6, 6, -2, 2),
    (3, -3, -5, 5), (-3, -5, 5, 3), (5, 3, -3, -5), (-5, 5, 3, -3),
    (0, 4, 8, -4), (4, 8, -4, 0), (8, -4, 0, 4), (-4, 0, 4, 8),
)


def routes():
    dst = np.zeros((2, CHIPS, N_TAU), np.int32)
    src = np.zeros((2, CHIPS, N_TAU), np.int32)
    column = np.zeros((2, CHIPS, CHIPS), np.int32)
    perms = []
    for j in range(2):
        for z in range(CHIPS):
            for k in range(N_TAU):
                to = (z + STEPS[(k + 8 * j) % N_TAU][z % 4]) % CHIPS
                dst[j, z, k] = to
                src[j, to, k] = z
                column[j, to, z] = k
        perms.append(
            [
                ((2 * z + core) * N_TAU + k, (2 * int(dst[j, z, k]) + (core ^ j)) * N_TAU + k)
                for z in range(CHIPS)
                for core in range(2)
                for k in range(N_TAU)
            ]
        )
    return dst, src, column, perms


DST, SRC, COLUMN, PERMS = routes()


def dot(a, b):
    return jnp.dot(a, b, preferred_element_type=F32)


VM = pl.BlockSpec(memory_space=pltpu.VMEM)
SM = pl.BlockSpec(memory_space=pltpu.SMEM)


def prepare_kernel(
    asked_ref, dst_ref, near_ref, away_ref, peers_ref, coeff_ref, gf_ref, gb_ref, send_ref, atom0_ref,
    atom1a_ref, atom1b_ref, wide
):
    p, k = lax.axis_index("pair"), lax.axis_index("tau")
    to = [2 * dst_ref[(j * CHIPS + p // 2) * N_TAU + k] + (p + j) % 2 for j in range(2)]
    atom0_ref[0] = coeff_ref[asked_ref[to[0]]]
    other = asked_ref[to[1]]
    atom1a_ref[0] = coeff_ref[other, :64]
    atom1b_ref[0] = coeff_ref[other, 64:]
    eye = lax.broadcasted_iota(jnp.int32, (32, 32), 0) == lax.broadcasted_iota(jnp.int32, (32, 32), 1)
    peers = peers_ref[...].astype(F32)

    def pick(table_ref):
        row = table_ref[pl.ds(p, 1), :]
        column = jnp.sum(jnp.where(eye, jnp.broadcast_to(row, (32, 32)), 0.0), axis=1, keepdims=True)
        return jnp.where(column == peers, 1.0, 0.0).astype(BF16)

    near, away = pick(near_ref), pick(away_ref)
    mine = jnp.concatenate([dot(near, gf_ref[...]), dot(near, gb_ref[...])], axis=0).astype(BF16)
    theirs = [dot(away, gf_ref[...]), dot(away, gb_ref[...])]
    for c in range(4):
        r = lax.broadcasted_iota(jnp.int32, (1024, 256), 0)
        q = lax.broadcasted_iota(jnp.int32, (1, 256), 1) + 256 * c
        source = (q % 32) * 32 + ((q // 32) % 4) * 8 + q // 128
        turn = jnp.where(r == source, 1.0, 0.0).astype(BF16)
        flipped = dot(mine, turn)
        for i in range(2):
            for kind in range(2):
                wide[:, 2 * c + i, kind * 128:(kind + 1) * 128] = flipped[
                    kind * 32:(kind + 1) * 32, i * 128:(i + 1) * 128
                ]
    for kind in range(2):
        for lo in range(8):
            wide[:, lo, 256 + kind * 128:256 + (kind + 1) * 128] = jnp.concatenate(
                [theirs[kind][:, (hi * 8 + lo) * 32:(hi * 8 + lo + 1) * 32] for hi in range(4)], axis=1
            )
    send_ref[...] = wide[...].astype(BF16)


def prepare(partner, send_atoms, coeff, fwd, bwd):
    sides = np.arange(N_PAIR) % 2
    near = np.zeros((N_PAIR, N_PAIR), np.float32)
    away = np.zeros((N_PAIR, N_PAIR), np.float32)
    for p in range(N_PAIR):
        for j in range(2):
            near[p, j::2] = 2 * SRC[j, p // 2] + (sides[p] ^ j)
            away[p, j::2] = 2 * DST[j, p // 2] + (sides[p] ^ j)
    return pl.pallas_call(
        prepare_kernel,
        in_specs=[SM] * 2 + [VM] * 6,
        out_specs=[VM] * 4,
        scratch_shapes=[pltpu.VMEM((32, 8, 512), F32)],
        out_shape=[
            jax.ShapeDtypeStruct((32, 8, 512), BF16),
            jax.ShapeDtypeStruct((1, AUX, 1024), BF16),
            jax.ShapeDtypeStruct((1, 64, 1024), BF16),
            jax.ShapeDtypeStruct((1, 64, 1024), BF16),
        ],
        cost_estimate=pl.CostEstimate(flops=200_000_000, bytes_accessed=3_000_000, transcendentals=0),
    )(
        send_atoms,
        jnp.asarray(DST.reshape(-1)),
        jnp.asarray(near),
        jnp.asarray(away),
        partner.reshape(1, N_PAIR),
        coeff,
        fwd,
        bwd,
    )


def turn_kernel(partner_ref, homes_ref, src_ref, coeff_ref, cin_ref):
    p, k = lax.axis_index("pair"), lax.axis_index("tau")
    for j in range(2):
        come = 2 * src_ref[(j * CHIPS + p // 2) * N_TAU + k]
        side = (p + j) % 2
        home = jnp.int32(0)
        for m in range(N_PAIR):
            home = jnp.where(partner_ref[m] == come + side, homes_ref[m], home)
        for c in range(4):
            cin_ref[j, :, c * 128:(c + 1) * 128] = coeff_ref[home, :, c * 256:(c + 1) * 256].astype(F32).T.astype(BF16)


def turn_home(partner, home_atom, coeff):
    return pl.pallas_call(
        turn_kernel,
        in_specs=[SM] * 3 + [VM],
        out_specs=VM,
        out_shape=jax.ShapeDtypeStruct((2, 256, 512), BF16),
        cost_estimate=pl.CostEstimate(flops=100_000_000, bytes_accessed=2_000_000, transcendentals=0),
    )(partner, home_atom, jnp.asarray(SRC.reshape(-1)), coeff)


UNROLL = 8


def expand(packed, repeat, dst):
    rows = packed.shape[0]
    i = lax.broadcasted_iota(jnp.int32, (128, 256), 0) % 32
    j = lax.broadcasted_iota(jnp.int32, (128, 256), 1)
    e = jnp.where(i == (j // 8 if repeat else j % 32), 1.0, 0.0).astype(BF16)
    keep = (lax.broadcasted_iota(jnp.int32, (64, 128), 0) // 16) == (lax.broadcasted_iota(jnp.int32, (64, 128), 1) // 32)
    rep = jnp.concatenate([packed.astype(F32)] * 8, axis=1)
    rep = jnp.where(keep[None], rep, 0.0).reshape(rows * 64, 128).astype(BF16)
    dst[...] = dot(rep, e).astype(BF16).reshape(rows, 64, 256)


def pipelined(fb, bb, cin_of, emit, s_a, s_b):
    count = fb.shape[0]
    row = lax.broadcasted_iota(jnp.int32, (64, 256), 0) // 8
    lane = lax.broadcasted_iota(jnp.int32, (64, 256), 1)
    mask_minor = jnp.where(row == lane // 32, 1.0, 0.0).astype(BF16)
    mask_major = jnp.where(row == lane % 8, 1.0, 0.0).astype(BF16)

    def spread(h, mask):
        return jnp.concatenate(
            [jnp.concatenate([h[a * 16:(a + 1) * 16]] * 4, axis=0) * mask for a in range(4)], axis=0
        )

    def first(t, buf):
        s1 = dot(spread(fb[t], mask_minor), cin_of(t)).astype(BF16)
        for h in range(4):
            for a in range(4):
                buf[a * 64:(a + 1) * 64, h * 128:(h + 1) * 128] = s1[h * 64:(h + 1) * 64, a * 128:(a + 1) * 128]

    def second(t, buf):
        m2 = spread(bb[t], mask_major)
        for h in range(2):
            emit(t, h, dot(m2, buf[:, h * 256:(h + 1) * 256]))

    first(0, s_a)

    def step(i, carry):
        for u in range(0, UNROLL, 2):
            t = UNROLL * i + u
            first(t + 1, s_b)
            second(t, s_a)
            first(jnp.minimum(t + 2, count - 1), s_a)
            second(t + 1, s_b)
        return carry

    lax.fori_loop(0, count // UNROLL, step, 0)


def own_kernel(cin_ref, own_ref, zo_ref, fb, bb, s_a, s_b):
    for j in range(2):
        part = slice(j * N_TAU, (j + 1) * N_TAU)
        expand(own_ref[:, j, :, 0:128], False, fb.at[part])
        expand(own_ref[:, j, :, 128:256], True, bb.at[part])

    def emit(t, h, z):
        zo_ref[t, :, h * 256:(h + 1) * 256] = z

    pipelined(fb, bb, lambda t: cin_ref[t // N_TAU], emit, s_a, s_b)


def own_half(cin, greens):
    return pl.pallas_call(
        own_kernel,
        in_specs=[VM] * 2,
        out_specs=VM,
        scratch_shapes=[pltpu.VMEM((2 * N_TAU, 64, 256), BF16)] * 2 + [pltpu.VMEM((256, 512), BF16)] * 2,
        out_shape=jax.ShapeDtypeStruct((2 * N_TAU, 256, 512), F32),
        compiler_params=pltpu.CompilerParams(vmem_limit_bytes=24 * 2**20),
        cost_estimate=pl.CostEstimate(flops=8_000_000_000, bytes_accessed=5_000_000, transcendentals=0),
    )(cin, greens)


def far_kernel(slot, cin_ref, far_ref, zo_ref, z_ref, fb, bb, s_a, s_b):
    expand(far_ref[:, :, 0:128], False, fb)
    expand(far_ref[:, :, 128:256], True, bb)

    def emit(t, h, z):
        z = z + zo_ref[slot * N_TAU + t, :, h * 256:(h + 1) * 256]
        z_ref[t, :, h * 512:h * 512 + 256] = z[:, :128].T.astype(BF16)
        z_ref[t, :, h * 512 + 256:h * 512 + 512] = z[:, 128:].T.astype(BF16)

    pipelined(fb, bb, lambda t: cin_ref[slot], emit, s_a, s_b)


def far_half(slot, cin, far, zo):
    return pl.pallas_call(
        functools.partial(far_kernel, slot),
        in_specs=[VM] * 3,
        out_specs=VM,
        scratch_shapes=[pltpu.VMEM((N_TAU, 64, 256), BF16)] * 2 + [pltpu.VMEM((256, 512), BF16)] * 2,
        out_shape=jax.ShapeDtypeStruct((N_TAU, AUX, 1024), BF16),
        compiler_params=pltpu.CompilerParams(vmem_limit_bytes=24 * 2**20),
        cost_estimate=pl.CostEstimate(flops=4_000_000_000, bytes_accessed=5_000_000, transcendentals=0),
    )(cin, far, zo)


def last_kernel(c0_ref, c1a_ref, c1b_ref, z0_ref, z1_ref, out_ref, cp):
    r = lax.broadcasted_iota(jnp.int32, (256, 256), 0)
    q = lax.broadcasted_iota(jnp.int32, (256, 256), 1)
    pm = jnp.where(q == (r % 32 // 8) * 64 + (r % 8) * 8 + r // 32, 1.0, 0.0).astype(BF16)
    for j in range(2):
        atom = c0_ref[0] if j == 0 else jnp.concatenate([c1a_ref[0], c1b_ref[0]], axis=0)
        turned = [dot(atom[:, a * 256:(a + 1) * 256], pm) for a in range(4)]
        for h in range(4):
            cp[j, :, h * 256:(h + 1) * 256] = jnp.concatenate(
                [turned[a][:, h * 64:(h + 1) * 64] for a in range(4)], axis=1
            ).astype(BF16)

    def step(i, carry):
        for j, ref in enumerate((z0_ref, z1_ref)):
            acc = lax.dot_general(
                ref[pl.ds(4 * i, 4)].reshape(4 * AUX, 1024),
                cp[j],
                (((1,), (1,)), ((), ())),
                preferred_element_type=F32,
            )
            out_ref[pl.ds(4 * i, 4), j] = (acc * (1.0 / AO)).astype(BF16).reshape(4, AUX, AUX)
        return carry

    lax.fori_loop(0, N_TAU // 4, step, 0)


def last_product(c0, c1a, c1b, z0, z1):
    return pl.pallas_call(
        last_kernel,
        in_specs=[VM] * 5,
        out_specs=VM,
        scratch_shapes=[pltpu.VMEM((2, AUX, 1024), BF16)],
        out_shape=jax.ShapeDtypeStruct((N_TAU, 2, AUX, AUX), BF16),
        compiler_params=pltpu.CompilerParams(vmem_limit_bytes=16 * 2**20),
        cost_estimate=pl.CostEstimate(flops=1_200_000_000, bytes_accessed=10_000_000, transcendentals=0),
    )(c0, c1a, c1b, z0, z1)


def finish_kernel(partner_ref, column_ref, in_ref, out_ref):
    base = pl.program_id(0) * 8
    p = lax.axis_index("pair")
    for i in range(8):
        other = partner_ref[base + i]
        j = (p + other) % 2
        place = 2 * column_ref[(j * CHIPS + p // 2) * CHIPS + other // 2] + j
        out_ref[i] = in_ref[place].astype(F32)


def finish(partner, tiles):
    return pl.pallas_call(
        finish_kernel,
        grid=(4,),
        in_specs=[SM, SM, VM],
        out_specs=pl.BlockSpec((8, AUX, AUX), lambda i: (i, 0, 0)),
        out_shape=jax.ShapeDtypeStruct((32, AUX, AUX), F32),
        compiler_params=pltpu.CompilerParams(vmem_limit_bytes=8 * 2**20),
        cost_estimate=pl.CostEstimate(flops=1_000_000, bytes_accessed=3_000_000, transcendentals=0),
    )(partner, jnp.asarray(COLUMN.reshape(-1)), tiles)


def exchange(x):
    return lax.all_to_all(x, "tau", split_axis=0, concat_axis=0, tiled=True)


def send_z(x, j):
    return lax.ppermute(x, BOTH, PERMS[j])


def body(coeff, green_fwd, green_bwd, home_atom, send_atoms, partner, mirror):
    send, atom0, atom1a, atom1b = prepare(partner, send_atoms, coeff, green_fwd[:, 0, :], green_bwd[:, 0, :])
    c0 = send_z(atom0, 0)
    c1a = send_z(atom1a, 1)
    c1b = send_z(atom1b, 1)
    greens = exchange(send).reshape(N_TAU, 2, 8, 512)
    cin = turn_home(partner, home_atom, coeff)
    far0 = send_z(greens[:, 0, :, 256:512], 0)
    far1 = send_z(greens[:, 1, :, 256:512], 1)
    zo = own_half(cin, greens)
    z0 = far_half(0, cin, far0, zo)
    z1 = far_half(1, cin, far1, zo)
    tiles = last_product(c0, c1a, c1b, z0, z1)
    back = exchange(tiles.reshape(32, AUX, AUX))
    return finish(partner, back).reshape(32, 1, AUX, AUX)


def solution(mesh):
    placed = (
        P("pair", None, None),
        P("pair", "tau", None),
        P("pair", "tau", None),
        P("pair"),
        P("pair"),
        P("pair"),
        P("pair"),
    )
    return jax.shard_map(
        body, mesh=mesh, in_specs=placed, out_specs=P("pair", "tau", None, None), check_vma=False
    )
```

```python
import functools

import jax
import jax.numpy as jnp
import numpy as np
from jax import lax
from jax.experimental import pallas as pl
from jax.experimental.pallas import tpu as pltpu
from jax.sharding import PartitionSpec as P


AUX = 128
AO = 32
CHIPS = 16
N_PAIR = 32
N_TAU = 16
F32 = jnp.float32
BF16 = jnp.bfloat16
BOTH = ("pair", "tau")


STEPS = (
    (1, 7, -7, -1), (7, -7, -1, 1), (-7, -1, 1, 7), (-1, 1, 7, -7),
    (2, -2, 6, -6), (-2, 2, -6, 6), (6, -6, 2, -2), (-6, 6, -2, 2),
    (3, -3, -5, 5), (-3, -5, 5, 3), (5, 3, -3, -5), (-5, 5, 3, -3),
    (0, 4, 8, -4), (4, 8, -4, 0), (8, -4, 0, 4), (-4, 0, 4, 8),
)


def routes():
    dst = np.zeros((2, CHIPS, N_TAU), np.int32)
    src = np.zeros((2, CHIPS, N_TAU), np.int32)
    column = np.zeros((2, CHIPS, CHIPS), np.int32)
    perms = []
    for j in range(2):
        for z in range(CHIPS):
            for k in range(N_TAU):
                to = (z + STEPS[(k + 8 * j) % N_TAU][z % 4]) % CHIPS
                dst[j, z, k] = to
                src[j, to, k] = z
                column[j, to, z] = k
        perms.append(
            [
                ((2 * z + core) * N_TAU + k, (2 * int(dst[j, z, k]) + (core ^ j)) * N_TAU + k)
                for z in range(CHIPS)
                for core in range(2)
                for k in range(N_TAU)
            ]
        )
    return dst, src, column, perms


DST, SRC, COLUMN, PERMS = routes()


def dot(a, b):
    return jnp.dot(a, b, preferred_element_type=F32)


VM = pl.BlockSpec(memory_space=pltpu.VMEM)
SM = pl.BlockSpec(memory_space=pltpu.SMEM)


def pick_kernel(asked_ref, dst_ref, coeff_ref, atom0_ref, atom1_ref):
    p, k = lax.axis_index("pair"), lax.axis_index("tau")
    for j, atom_ref in enumerate((atom0_ref, atom1_ref)):
        to = 2 * dst_ref[(j * CHIPS + p // 2) * N_TAU + k] + (p + j) % 2
        atom_ref[0] = coeff_ref[asked_ref[to]]


def pick_atoms(send_atoms, coeff):
    return pl.pallas_call(
        pick_kernel,
        in_specs=[SM] * 2 + [VM],
        out_specs=[VM] * 2,
        out_shape=[jax.ShapeDtypeStruct((1, AUX, 1024), BF16)] * 2,
        cost_estimate=pl.CostEstimate(flops=1_000_000, bytes_accessed=2_000_000, transcendentals=0),
    )(send_atoms, jnp.asarray(DST.reshape(-1)), coeff)


def prepare_kernel(near_ref, away_ref, peers_ref, gf_ref, gb_ref, send_ref, wide):
    p = lax.axis_index("pair")
    eye = lax.broadcasted_iota(jnp.int32, (32, 32), 0) == lax.broadcasted_iota(jnp.int32, (32, 32), 1)
    peers = peers_ref[...].astype(F32)

    def pick(table_ref):
        row = table_ref[pl.ds(p, 1), :]
        column = jnp.sum(jnp.where(eye, jnp.broadcast_to(row, (32, 32)), 0.0), axis=1, keepdims=True)
        return jnp.where(column == peers, 1.0, 0.0).astype(BF16)

    near, away = pick(near_ref), pick(away_ref)
    mine = jnp.concatenate([dot(near, gf_ref[...]), dot(near, gb_ref[...])], axis=0).astype(BF16)
    theirs = [dot(away, gf_ref[...]), dot(away, gb_ref[...])]
    for c in range(4):
        r = lax.broadcasted_iota(jnp.int32, (1024, 256), 0)
        q = lax.broadcasted_iota(jnp.int32, (1, 256), 1) + 256 * c
        source = (q % 32) * 32 + ((q // 32) % 4) * 8 + q // 128
        turn = jnp.where(r == source, 1.0, 0.0).astype(BF16)
        flipped = dot(mine, turn)
        for i in range(2):
            for kind in range(2):
                wide[:, 2 * c + i, kind * 128:(kind + 1) * 128] = flipped[
                    kind * 32:(kind + 1) * 32, i * 128:(i + 1) * 128
                ]
    for kind in range(2):
        for lo in range(8):
            wide[:, lo, 256 + kind * 128:256 + (kind + 1) * 128] = jnp.concatenate(
                [theirs[kind][:, (hi * 8 + lo) * 32:(hi * 8 + lo + 1) * 32] for hi in range(4)], axis=1
            )
    send_ref[...] = wide[...].astype(BF16)


def prepare(partner, fwd, bwd):
    sides = np.arange(N_PAIR) % 2
    near = np.zeros((N_PAIR, N_PAIR), np.float32)
    away = np.zeros((N_PAIR, N_PAIR), np.float32)
    for p in range(N_PAIR):
        for j in range(2):
            near[p, j::2] = 2 * SRC[j, p // 2] + (sides[p] ^ j)
            away[p, j::2] = 2 * DST[j, p // 2] + (sides[p] ^ j)
    return pl.pallas_call(
        prepare_kernel,
        in_specs=[VM] * 5,
        out_specs=VM,
        scratch_shapes=[pltpu.VMEM((32, 8, 512), F32)],
        out_shape=jax.ShapeDtypeStruct((32, 8, 512), BF16),
        cost_estimate=pl.CostEstimate(flops=200_000_000, bytes_accessed=1_000_000, transcendentals=0),
    )(jnp.asarray(near), jnp.asarray(away), partner.reshape(1, N_PAIR), fwd, bwd)


def turn_kernel(partner_ref, homes_ref, src_ref, coeff_ref, cin_ref):
    p, k = lax.axis_index("pair"), lax.axis_index("tau")
    for j in range(2):
        come = 2 * src_ref[(j * CHIPS + p // 2) * N_TAU + k]
        side = (p + j) % 2
        home = jnp.int32(0)
        for m in range(N_PAIR):
            home = jnp.where(partner_ref[m] == come + side, homes_ref[m], home)
        for c in range(4):
            cin_ref[j, :, c * 128:(c + 1) * 128] = coeff_ref[home, :, c * 256:(c + 1) * 256].astype(F32).T.astype(BF16)


def turn_home(partner, home_atom, coeff):
    return pl.pallas_call(
        turn_kernel,
        in_specs=[SM] * 3 + [VM],
        out_specs=VM,
        out_shape=jax.ShapeDtypeStruct((2, 256, 512), BF16),
        cost_estimate=pl.CostEstimate(flops=100_000_000, bytes_accessed=2_000_000, transcendentals=0),
    )(partner, home_atom, jnp.asarray(SRC.reshape(-1)), coeff)


UNROLL = 8


def expand(packed, repeat, dst):
    rows = packed.shape[0]
    i = lax.broadcasted_iota(jnp.int32, (128, 256), 0) % 32
    j = lax.broadcasted_iota(jnp.int32, (128, 256), 1)
    e = jnp.where(i == (j // 8 if repeat else j % 32), 1.0, 0.0).astype(BF16)
    keep = (lax.broadcasted_iota(jnp.int32, (64, 128), 0) // 16) == (lax.broadcasted_iota(jnp.int32, (64, 128), 1) // 32)
    rep = jnp.concatenate([packed.astype(F32)] * 8, axis=1)
    rep = jnp.where(keep[None], rep, 0.0).reshape(rows * 64, 128).astype(BF16)
    dst[...] = dot(rep, e).astype(BF16).reshape(rows, 64, 256)


def pipelined(fb, bb, cin_of, emit, s_a, s_b):
    count = fb.shape[0]
    row = lax.broadcasted_iota(jnp.int32, (64, 256), 0) // 8
    lane = lax.broadcasted_iota(jnp.int32, (64, 256), 1)
    mask_minor = jnp.where(row == lane // 32, 1.0, 0.0).astype(BF16)
    mask_major = jnp.where(row == lane % 8, 1.0, 0.0).astype(BF16)

    def spread(h, mask):
        return jnp.concatenate(
            [jnp.concatenate([h[a * 16:(a + 1) * 16]] * 4, axis=0) * mask for a in range(4)], axis=0
        )

    def first(t, buf):
        s1 = dot(spread(fb[t], mask_minor), cin_of(t)).astype(BF16)
        for h in range(4):
            for a in range(4):
                buf[a * 64:(a + 1) * 64, h * 128:(h + 1) * 128] = s1[h * 64:(h + 1) * 64, a * 128:(a + 1) * 128]

    def second(t, buf):
        m2 = spread(bb[t], mask_major)
        for h in range(2):
            emit(t, h, dot(m2, buf[:, h * 256:(h + 1) * 256]))

    first(0, s_a)

    def step(i, carry):
        for u in range(0, UNROLL, 2):
            t = UNROLL * i + u
            first(t + 1, s_b)
            second(t, s_a)
            first(jnp.minimum(t + 2, count - 1), s_a)
            second(t + 1, s_b)
        return carry

    lax.fori_loop(0, count // UNROLL, step, 0)


def own_kernel(cin_ref, own_ref, zo_ref, fb, bb, s_a, s_b):
    for j in range(2):
        part = slice(j * N_TAU, (j + 1) * N_TAU)
        expand(own_ref[:, j, :, 0:128], False, fb.at[part])
        expand(own_ref[:, j, :, 128:256], True, bb.at[part])

    def emit(t, h, z):
        zo_ref[t, :, h * 256:(h + 1) * 256] = z

    pipelined(fb, bb, lambda t: cin_ref[t // N_TAU], emit, s_a, s_b)


def own_half(cin, greens):
    return pl.pallas_call(
        own_kernel,
        in_specs=[VM] * 2,
        out_specs=VM,
        scratch_shapes=[pltpu.VMEM((2 * N_TAU, 64, 256), BF16)] * 2 + [pltpu.VMEM((256, 512), BF16)] * 2,
        out_shape=jax.ShapeDtypeStruct((2 * N_TAU, 256, 512), F32),
        compiler_params=pltpu.CompilerParams(vmem_limit_bytes=24 * 2**20),
        cost_estimate=pl.CostEstimate(flops=8_000_000_000, bytes_accessed=5_000_000, transcendentals=0),
    )(cin, greens)


def far_kernel(slot, cin_ref, far_ref, zo_ref, z_ref, fb, bb, s_a, s_b):
    expand(far_ref[:, :, 0:128], False, fb)
    expand(far_ref[:, :, 128:256], True, bb)

    def emit(t, h, z):
        z = z + zo_ref[slot * N_TAU + t, :, h * 256:(h + 1) * 256]
        z_ref[t, :, h * 512:h * 512 + 256] = z[:, :128].T.astype(BF16)
        z_ref[t, :, h * 512 + 256:h * 512 + 512] = z[:, 128:].T.astype(BF16)

    pipelined(fb, bb, lambda t: cin_ref[slot], emit, s_a, s_b)


def far_half(slot, cin, far, zo):
    return pl.pallas_call(
        functools.partial(far_kernel, slot),
        in_specs=[VM] * 3,
        out_specs=VM,
        scratch_shapes=[pltpu.VMEM((N_TAU, 64, 256), BF16)] * 2 + [pltpu.VMEM((256, 512), BF16)] * 2,
        out_shape=jax.ShapeDtypeStruct((N_TAU, AUX, 1024), BF16),
        compiler_params=pltpu.CompilerParams(vmem_limit_bytes=24 * 2**20),
        cost_estimate=pl.CostEstimate(flops=4_000_000_000, bytes_accessed=5_000_000, transcendentals=0),
    )(cin, far, zo)


def last_kernel(c0_ref, c1_ref, z0_ref, z1_ref, out_ref, cp):
    r = lax.broadcasted_iota(jnp.int32, (256, 256), 0)
    q = lax.broadcasted_iota(jnp.int32, (256, 256), 1)
    pm = jnp.where(q == (r % 32 // 8) * 64 + (r % 8) * 8 + r // 32, 1.0, 0.0).astype(BF16)
    for j, ref in enumerate((c0_ref, c1_ref)):
        turned = [dot(ref[0, :, a * 256:(a + 1) * 256], pm) for a in range(4)]
        for h in range(4):
            cp[j, :, h * 256:(h + 1) * 256] = jnp.concatenate(
                [turned[a][:, h * 64:(h + 1) * 64] for a in range(4)], axis=1
            ).astype(BF16)

    def step(i, carry):
        for j, ref in enumerate((z0_ref, z1_ref)):
            acc = lax.dot_general(
                ref[pl.ds(4 * i, 4)].reshape(4 * AUX, 1024),
                cp[j],
                (((1,), (1,)), ((), ())),
                preferred_element_type=F32,
            )
            out_ref[pl.ds(4 * i, 4), j] = (acc * (1.0 / AO)).astype(BF16).reshape(4, AUX, AUX)
        return carry

    lax.fori_loop(0, N_TAU // 4, step, 0)


def last_product(c0, c1, z0, z1):
    return pl.pallas_call(
        last_kernel,
        in_specs=[VM] * 4,
        out_specs=VM,
        scratch_shapes=[pltpu.VMEM((2, AUX, 1024), BF16)],
        out_shape=jax.ShapeDtypeStruct((N_TAU, 2, AUX, AUX), BF16),
        compiler_params=pltpu.CompilerParams(vmem_limit_bytes=16 * 2**20),
        cost_estimate=pl.CostEstimate(flops=1_200_000_000, bytes_accessed=10_000_000, transcendentals=0),
    )(c0, c1, z0, z1)


def finish_kernel(partner_ref, column_ref, in_ref, out_ref):
    base = pl.program_id(0) * 8
    p = lax.axis_index("pair")
    for i in range(8):
        other = partner_ref[base + i]
        j = (p + other) % 2
        place = 2 * column_ref[(j * CHIPS + p // 2) * CHIPS + other // 2] + j
        out_ref[i] = in_ref[place].astype(F32)


def finish(partner, tiles):
    return pl.pallas_call(
        finish_kernel,
        grid=(4,),
        in_specs=[SM, SM, VM],
        out_specs=pl.BlockSpec((8, AUX, AUX), lambda i: (i, 0, 0)),
        out_shape=jax.ShapeDtypeStruct((32, AUX, AUX), F32),
        compiler_params=pltpu.CompilerParams(vmem_limit_bytes=8 * 2**20),
        cost_estimate=pl.CostEstimate(flops=1_000_000, bytes_accessed=3_000_000, transcendentals=0),
    )(partner, jnp.asarray(COLUMN.reshape(-1)), tiles)


def exchange(x):
    return lax.all_to_all(x, "tau", split_axis=0, concat_axis=0, tiled=True)


def send_z(x, j):
    return lax.ppermute(x, BOTH, PERMS[j])


def body(coeff, green_fwd, green_bwd, home_atom, send_atoms, partner, mirror):
    atom0, atom1 = pick_atoms(send_atoms, coeff)
    send = prepare(partner, green_fwd[:, 0, :], green_bwd[:, 0, :])
    c0 = send_z(atom0, 0)
    c1 = send_z(atom1, 1)
    greens = exchange(send).reshape(N_TAU, 2, 8, 512)
    cin = turn_home(partner, home_atom, coeff)
    far0 = send_z(greens[:, 0, :, 256:512], 0)
    far1 = send_z(greens[:, 1, :, 256:512], 1)
    zo = own_half(cin, greens)
    z0 = far_half(0, cin, far0, zo)
    z1 = far_half(1, cin, far1, zo)
    tiles = last_product(c0, c1, z0, z1)
    back = exchange(tiles.reshape(32, AUX, AUX))
    return finish(partner, back).reshape(32, 1, AUX, AUX)


def solution(mesh):
    placed = (
        P("pair", None, None),
        P("pair", "tau", None),
        P("pair", "tau", None),
        P("pair"),
        P("pair"),
        P("pair"),
        P("pair"),
    )
    return jax.shard_map(
        body, mesh=mesh, in_specs=placed, out_specs=P("pair", "tau", None, None), check_vma=False
    )
```
